512 devices in a mesh: area: 64 (over y, x, core), snap: 8 (over z).
Axes of the slice: x: 4, y: 8, z: 8, core: 2. Of those that a mesh axis runs over, the one named last changes fastest.
Arguments:
- phasor_readings: float32 [256, 131072], P('snap', 'area')
- reading_error_spread: float32 [131072], P('area'), may hold values from 1 to 100
- starting_voltages: float32 [256, 131072], P('snap', 'area'), may hold values from -6 to 6
- derivative_pieces: bfloat16 [1024, 4, 128, 128], P('area'), may hold values from -0.25 to 0.25
- derivative_tile_position: int32 [64, 16, 4], P('area'), may hold values from 0 to 23, as said below
- frontier_voltage_pieces: int32 [64, 2, 4], P('area'), may hold values from -1 to 15, as said below
- holder_line_order: int32 [64, 64, 64], P('area'), may hold values from -1 to 2047, as said below
- hub_line_order: int32 [64, 64, 64], P('area'), may hold values from -1 to 2047, as said below
- reciprocal_normal_operator: bfloat16 [131072, 2048], P(('area', 'snap'))
Outputs:
- state: float32 [256, 131072], P('snap', 'area')
The draws below stay inside these ranges and needn't reach their ends.
Inputs may be any that keep to these rules, and one draw needn't show every extreme that they name: holder_line_order[d, c] lists the owner rows of area d that concentrator c handles, at most 64 of them, then -1; every owner row appears exactly once over all concentrators; some pair holds exactly 64. hub_line_order[c, d] lists the rows of concentrator c matching holder_line_order[d, c] entry by entry, with -1 at the same places; every concentrator row appears exactly once. `derivative_tile_position`: the 4 slots of one measurement block are distinct. frontier_voltage_pieces[a, 0] lists distinct blocks sent to area a - 1 and frontier_voltage_pieces[a, 1] those sent to area a + 1, 1 to 4 of them then -1; the list of area 0 toward lower and of the last area toward upper are all -1; some list holds 4.
All inputs are finite; a program needn't handle non-finite values.
Results may differ from the reference program's by a relative error of at most 0.0022.
Values may be sent and summed in bfloat16 or wider, within the bound.
A program may use at most 64 MiB of HBM per device.

```python
import math
import jax
import jax.numpy as jnp
from jax import lax

NS = 2048
BLK = 128
MEASURE_BLOCKS = 16
TOUCHED_BLOCKS = 4
TIES = 4
ITERS = 2
NB = 16
SLOT_COUNT = 24
READING_LINES = 2048
CONTROL_AREAS = 64
SNAPS = 256
CAP = 64


def route_tables(key):
    base = jax.random.fold_in(key, 11)
    key_pair, key_order, key_cycle, key_owner, key_conc = jax.random.split(base, 5)
    half = CAP // 2
    paired = jax.random.randint(key_pair, (CONTROL_AREAS // 2,), 0, half + 1).at[0].set(half)
    amounts = jnp.stack([half + paired, half - paired], axis=1).reshape(CONTROL_AREAS)
    amounts = amounts[jax.random.permutation(key_order, CONTROL_AREAS)]
    cycle = jax.random.permutation(key_cycle, CONTROL_AREAS)
    counts = amounts[(cycle[None, :] - cycle[:, None]) % CONTROL_AREAS]
    places = jnp.arange(CAP)
    owner_perm = jax.vmap(lambda subset_key: jax.random.permutation(subset_key, READING_LINES))(jax.random.split(key_owner, CONTROL_AREAS))
    conc_perm = jax.vmap(lambda subset_key: jax.random.permutation(subset_key, READING_LINES))(jax.random.split(key_conc, CONTROL_AREAS))
    owner_start = jnp.cumsum(counts, axis=0) - counts
    conc_start = jnp.cumsum(counts, axis=1) - counts
    owner_pos = jnp.clip(owner_start.T[:, :, None] + places[None, None, :], 0, READING_LINES - 1)
    conc_pos = jnp.clip(conc_start[:, :, None] + places[None, None, :], 0, READING_LINES - 1)
    owner_rows = jax.vmap(lambda perm, where_at: perm[where_at])(owner_perm, owner_pos)
    conc_rows = jax.vmap(lambda perm, where_at: perm[where_at])(conc_perm, conc_pos)
    owner_table = jnp.where(places[None, None, :] < counts.T[:, :, None], owner_rows, -1)
    conc_table = jnp.where(places[None, None, :] < counts[:, :, None], conc_rows, -1)
    return (owner_table.astype(jnp.int32), conc_table.astype(jnp.int32))


def draw_holder_line_order(key, part):
    return route_tables(key)[0]


def draw_hub_line_order(key, part):
    return route_tables(key)[1]


def draw_frontier_voltage_pieces(key, part):
    key_perm, key_count, key_full = jax.random.split(jax.random.fold_in(key, 23), 3)
    permutation_list = jax.vmap(lambda subset_key: jax.random.permutation(subset_key, NB))(jax.random.split(key_perm, CONTROL_AREAS * 2))
    permutation_list = permutation_list[:, :TIES].reshape(CONTROL_AREAS, 2, TIES)
    counts = jax.random.randint(key_count, (CONTROL_AREAS, 2), 1, TIES + 1)
    full_area = jax.random.randint(key_full, (), 1, CONTROL_AREAS - 1)
    counts = counts.at[full_area, 0].set(TIES)
    counts = counts.at[0, 0].set(0).at[CONTROL_AREAS - 1, 1].set(0)
    live = jnp.arange(TIES)[None, None, :] < counts[:, :, None]
    return jnp.where(live, permutation_list, -1).astype(jnp.int32)


def draw_derivative_tile_position(key, part):
    split_keys = jax.random.split(jax.random.fold_in(key, 31), CONTROL_AREAS * MEASURE_BLOCKS)
    permutation_list = jax.vmap(lambda subset_key: jax.random.permutation(subset_key, SLOT_COUNT))(split_keys)[:, :TOUCHED_BLOCKS]
    return permutation_list.reshape(CONTROL_AREAS, MEASURE_BLOCKS, TOUCHED_BLOCKS).astype(jnp.int32)


def draw_reciprocal_normal_operator(key, part):
    key_noise, key_diag = jax.random.split(jax.random.fold_in(key, 41))
    total_rows = CONTROL_AREAS * NS
    noise = jax.random.normal(key_noise, (total_rows, NS), jnp.float32)
    diagonal = jax.random.uniform(key_diag, (total_rows, 1), jnp.float32, 2.0, 6.0)
    position = (jnp.arange(total_rows) % NS)[:, None]
    matrix = noise * (2.5 / math.sqrt(NS)) + jnp.where(position == jnp.arange(NS)[None, :], diagonal, 0.0)
    return matrix.astype(jnp.bfloat16)


def draw_phasor_readings(key, part):
    key_base, key_row, key_col = jax.random.split(jax.random.fold_in(key, 53), 3)
    columns = CONTROL_AREAS * READING_LINES
    row_scale = jnp.exp(jax.random.uniform(key_row, (1, columns), jnp.float32, math.log(0.5), math.log(5.0)))
    ramp = jnp.arange(SNAPS, dtype=jnp.float32) / max(SNAPS - 1, 1)
    jitter = jax.random.uniform(key_col, (SNAPS, 1), jnp.float32, 0.8, 1.25)
    col_scale = jnp.exp(ramp * math.log(10.0))[:, None] * jitter
    base = jax.random.normal(key_base, (SNAPS, columns), jnp.float32)
    return base * row_scale * col_scale


def block_scale(rng, dims, cuts, least, high):
    loudness = 1.0
    for dim, shards_of in cuts:
        heights = jax.random.uniform(jax.random.fold_in(jax.random.fold_in(rng, 6), dim), (shards_of,), jnp.float32, least / len(cuts), high / len(cuts))
        loudness = loudness * jnp.repeat(jnp.exp(heights), dims[dim] // shards_of).reshape((-1,) + (1,) * (len(dims) - 1 - dim))
    return loudness


def normal_values(stream_key, dims, scale, reach, shards=(), kind=jnp.bfloat16):
    result = jax.random.normal(stream_key, dims, jnp.float32) * scale
    if len(shards) > 0:
        result = block_scale(stream_key, dims, shards, -0.22, 0.18) * result
    return jnp.clip(result, min=-reach, max=reach).astype(kind)


def setup_inputs(seed: int = 0) -> dict:
    key_of = jax.random.split(jax.random.key(seed), 10)
    return {
        "phasor_readings": draw_phasor_readings(jax.random.fold_in(key_of[9], 71), 0),
        "reading_error_spread": jnp.clip(jnp.exp(math.log(100.0) - 4.6051702 * jax.random.uniform(key_of[1], (CONTROL_AREAS * READING_LINES,), jnp.float32) ** block_scale(key_of[1], (CONTROL_AREAS * READING_LINES,), ((0, 64),), -0.2, 0.2)), 1.0, 100.0),
        "starting_voltages": normal_values(key_of[2], (SNAPS, CONTROL_AREAS * NS), 1.0, 6.0, ((0, 8), (1, 64)), jnp.float32),
        "derivative_pieces": normal_values(key_of[3], (CONTROL_AREAS * MEASURE_BLOCKS, TOUCHED_BLOCKS, BLK, BLK), (TOUCHED_BLOCKS * BLK) ** -0.5, 0.25, ((0, 64),)),
        "derivative_tile_position": draw_derivative_tile_position(jax.random.fold_in(key_of[9], 71), 0),
        "frontier_voltage_pieces": draw_frontier_voltage_pieces(jax.random.fold_in(key_of[9], 71), 0),
        "holder_line_order": draw_holder_line_order(jax.random.fold_in(key_of[9], 71), 0),
        "hub_line_order": draw_hub_line_order(jax.random.fold_in(key_of[9], 71), 0),
        "reciprocal_normal_operator": draw_reciprocal_normal_operator(jax.random.fold_in(key_of[9], 71), 0),
    }


HIGHEST_PRECISION = lax.Precision.HIGHEST


def take_blocks(blocks, listing):
    safe = jnp.maximum(listing, 0)
    taken = jax.vmap(lambda values, where_at: values[:, where_at])(blocks, safe)
    return jnp.where((listing >= 0)[:, None, :, None], taken, 0.0)


def put_blocks(values, listing):
    onehot_table = (listing[:, :, None] == jnp.arange(NB, dtype=jnp.int32)[None, None, :]).astype(jnp.float32)
    return jnp.einsum("astc,atb->asbc", values, onehot_table, precision=HIGHEST_PRECISION)


def reference(phasor_readings, reading_error_spread, starting_voltages, derivative_pieces, derivative_tile_position, frontier_voltage_pieces, holder_line_order, hub_line_order, reciprocal_normal_operator):
    region_sequence = holder_line_order.shape[0]
    capture_number = phasor_readings.shape[0]
    valid = holder_line_order >= 0
    owner_index = jnp.arange(region_sequence, dtype=jnp.int32)[:, None, None] * READING_LINES + holder_line_order
    conc_swap = jnp.transpose(hub_line_order, (1, 0, 2))
    conc_index = jnp.arange(region_sequence, dtype=jnp.int32)[None, :, None] * READING_LINES + conc_swap
    target = jnp.where(valid, owner_index, region_sequence * READING_LINES).reshape(-1).astype(jnp.int32)
    provider_lines = jnp.zeros((region_sequence * READING_LINES,), jnp.int32).at[target].set(conc_index.reshape(-1).astype(jnp.int32), mode="drop")
    observed_quantities = jnp.transpose(phasor_readings[:, provider_lines].reshape(capture_number, region_sequence, READING_LINES), (1, 0, 2))
    noise_variance = reading_error_spread[provider_lines].reshape(region_sequence, READING_LINES)
    tiles = derivative_pieces.reshape(region_sequence, MEASURE_BLOCKS, TOUCHED_BLOCKS, BLK, BLK)
    gains = reciprocal_normal_operator.reshape(region_sequence, NS, NS)
    current = jnp.transpose(starting_voltages.reshape(capture_number, region_sequence, NB, BLK), (1, 0, 2, 3))
    empty = jnp.zeros((1, capture_number, TIES, BLK), jnp.float32)
    slot_lookup = (derivative_tile_position.reshape(region_sequence, MEASURE_BLOCKS * TOUCHED_BLOCKS)[:, :, None] == jnp.arange(SLOT_COUNT, dtype=jnp.int32)[None, None, :]).astype(jnp.float32)

    def predict(inputs):
        tile, slot_column_index, augmented = inputs
        chosen = augmented[:, slot_column_index].astype(jnp.float32)
        return jnp.einsum("jkrc,sjkc->sjr", tile.astype(jnp.float32), chosen, precision=HIGHEST_PRECISION).reshape(capture_number, READING_LINES)

    def pull(inputs):
        tile, onehot_table, weighted = inputs
        tile_grad = jnp.einsum("jkrc,sjr->sjkc", tile.astype(jnp.float32), weighted.reshape(capture_number, MEASURE_BLOCKS, BLK).astype(jnp.float32), precision=HIGHEST_PRECISION)
        return jnp.einsum("sxc,xn->snc", tile_grad.reshape(capture_number, MEASURE_BLOCKS * TOUCHED_BLOCKS, BLK), onehot_table, precision=HIGHEST_PRECISION)

    def apply_gain(inputs):
        gradient, matrix = inputs
        return jnp.dot(gradient, matrix.T, preferred_element_type=jnp.float32)

    for step_index in range(ITERS):
        from_below = jnp.concatenate([empty, take_blocks(current, frontier_voltage_pieces[:, 1])[:-1]], axis=0)
        from_above = jnp.concatenate([take_blocks(current, frontier_voltage_pieces[:, 0])[1:], empty], axis=0)
        augmented = jnp.concatenate([current, from_below, from_above], axis=2).astype(jnp.bfloat16)
        predicted = lax.map(predict, (tiles, derivative_tile_position, augmented))
        residual_rows = observed_quantities - predicted
        spread = jnp.sum(residual_rows * residual_rows, axis=1) / capture_number
        weighted = (residual_rows / (noise_variance + spread)[:, None, :]).astype(jnp.bfloat16)
        slot_grad = lax.map(pull, (tiles, slot_lookup, weighted))
        below_slots = slot_grad[:, :, NB:NB + TIES]
        above_slots = slot_grad[:, :, NB + TIES:]
        back_upper = jnp.concatenate([below_slots[1:], empty], axis=0)
        back_lower = jnp.concatenate([empty, above_slots[:-1]], axis=0)
        gradient = slot_grad[:, :, :NB] + put_blocks(back_upper, frontier_voltage_pieces[:, 1]) + put_blocks(back_lower, frontier_voltage_pieces[:, 0])
        flat_grad = gradient.reshape(region_sequence, capture_number, NS).astype(jnp.bfloat16)
        update = lax.map(apply_gain, (flat_grad, gains))
        current = current + update.reshape(region_sequence, capture_number, NB, BLK)
    return jnp.transpose(current.reshape(region_sequence, capture_number, NS), (1, 0, 2)).reshape(capture_number, region_sequence * NS)
```

```python
import functools

import jax
import jax.numpy as jnp
from jax import lax
from jax.experimental import pallas as pl
from jax.experimental.pallas import tpu as pltpu
from jax.sharding import PartitionSpec as P

ITERS = 2
LANES = 128
MESH = pl.DeviceIdType.MESH
NT = (((1,), (1,)), ((), ()))


def step_kernel(
    dims,
    z_ref,
    var_ref,
    x_ref,
    tiles_hbm,
    pos_ref,
    ties_ref,
    holder_ref,
    hub_ref,
    gain_hbm,
    out_ref,
    tiles,
    gain,
    gain_t,
    tile_index,
    table,
    zs,
    zr,
    vs,
    vr,
    arrived,
    inv_q,
    inv_lane,
    z_own,
    v_own,
    aug,
    fs,
    fr,
    resid,
    ssr,
    wgt,
    grads,
    bs,
    br,
    gath,
    us,
    ur,
    local_sem,
    z_send,
    z_recv,
    v_send,
    v_recv,
    f_send,
    f_recv,
    s_send,
    s_recv,
    b_send,
    b_recv,
    ring_send,
    ring_recv,
    u_send,
    u_recv,
):
    areas, peers, snaps, nb, mb, touched, ties, cap = dims
    half = snaps // 2
    chunks = areas * cap // LANES
    rows = nb * LANES // peers
    units = nb // 2
    piece_units = 2
    pieces = units // piece_units
    reach = peers // 2
    slots = nb + 2 * ties
    all_tiles = mb * touched
    snaps_all = snaps * peers
    f32, bf16, i32 = jnp.float32, jnp.bfloat16, jnp.int32

    a = lax.axis_index("area")
    s = lax.axis_index("snap")
    has_lower = a > 0
    has_upper = a < areas - 1

    tiles_copy = pltpu.make_async_copy(
        tiles_hbm, tiles.at[pl.ds(0, all_tiles)], local_sem.at[0]
    )
    gain_copy = pltpu.make_async_copy(gain_hbm, gain, local_sem.at[1])
    tiles_copy.start()
    gain_copy.start()

    barrier = pltpu.get_barrier_semaphore()

    def greet_area(i, carry):
        pl.semaphore_signal(
            barrier, inc=1, device_id=(lax.rem(a + i, areas), s), device_id_type=MESH
        )
        return carry

    def greet_snap(i, carry):
        pl.semaphore_signal(
            barrier, inc=1, device_id=(a, lax.rem(s + i, peers)), device_id_type=MESH
        )
        return carry

    lax.fori_loop(1, areas, greet_area, 0)
    lax.fori_loop(1, peers, greet_snap, 0)

    lane_a = lax.broadcasted_iota(i32, (areas, LANES), 1)
    for index, listing in enumerate((hub_ref, holder_ref)):
        both = jnp.concatenate([listing[...], listing[...]], axis=1)
        table[index] = both
    for block in range(nb):
        aug[block] = x_ref[:, block * LANES : (block + 1) * LANES].astype(bf16)
    aug[slots] = jnp.zeros((snaps, LANES), bf16)
    for step in range(ITERS):
        for side in range(2):
            br[step, side, ties] = jnp.zeros((snaps, LANES), f32)

    @pl.when(jnp.logical_not(has_lower))
    def _():
        for t in range(ties):
            aug[nb + t] = jnp.zeros((snaps, LANES), bf16)
            for step in range(ITERS):
                br[step, 0, t] = jnp.zeros((snaps, LANES), f32)

    @pl.when(jnp.logical_not(has_upper))
    def _():
        for t in range(ties):
            aug[nb + ties + t] = jnp.zeros((snaps, LANES), bf16)
            for step in range(ITERS):
                br[step, 1, t] = jnp.zeros((snaps, LANES), f32)

    pl.semaphore_wait(barrier, areas - 1 + peers - 1)

    def frontier_copy(step, side):
        return pltpu.make_async_remote_copy(
            src_ref=fs.at[step, side],
            dst_ref=fr.at[step, 1 - side],
            send_sem=f_send.at[step, side],
            recv_sem=f_recv.at[step, side],
            device_id=(a - 1 if side == 0 else a + 1, s),
            device_id_type=MESH,
        )

    def frontier_start(step):
        for side in range(2):
            for t in range(ties):
                entry = ties_ref[side, t]
                fs[step, side, t] = aug[jnp.where(entry >= 0, entry, slots)]

        @pl.when(has_lower)
        def _():
            frontier_copy(step, 0).start()

        @pl.when(has_upper)
        def _():
            frontier_copy(step, 1).start()

    def frontier_wait(step):
        @pl.when(has_lower)
        def _():
            frontier_copy(step, 1).wait_recv()
            for t in range(ties):
                aug[nb + t] = fr[step, 0, t]

        @pl.when(has_upper)
        def _():
            frontier_copy(step, 0).wait_recv()
            for t in range(ties):
                aug[nb + ties + t] = fr[step, 1, t]

    frontier_start(0)

    def table_row(index, q):
        even = table[index, pl.ds(2 * q, 1), :]
        odd = table[index, pl.ds(2 * q + 1, 1), :]
        lane = lax.broadcasted_iota(i32, (1, LANES), 1)
        return jnp.where(lane < cap, even, odd)

    lane_h = lax.broadcasted_iota(i32, (half, LANES), 1)

    def route_out(i, carry):
        q = lax.rem(lax.div(a, 2) + i, chunks)
        where_at = table_row(0, q)
        block_of = lax.shift_right_arithmetic(where_at, 7)
        lane_of = where_at & (LANES - 1)
        lanes = jnp.broadcast_to(lane_of, (snaps, LANES))
        from_block = jnp.broadcast_to(block_of, (snaps, LANES))
        taken = jnp.zeros((snaps, LANES), f32)
        for block in range(mb):
            found = jnp.take_along_axis(
                z_ref[:, block * LANES : (block + 1) * LANES], lanes, axis=1
            )
            taken = jnp.where(from_block == block, found, taken)
        low, high = taken[:half], taken[half:]
        zs[2 * q] = jnp.where(lane_h < cap, low, pltpu.roll(high, cap, 1))
        zs[2 * q + 1] = jnp.where(lane_h < cap, pltpu.roll(low, cap, 1), high)
        var_found = jnp.take_along_axis(
            var_ref[...], jnp.broadcast_to(lane_of, (mb, LANES)), axis=1
        )
        var_rows = lax.broadcasted_iota(i32, (mb, LANES), 0)
        vs[q] = jnp.sum(
            jnp.where(var_rows == jnp.broadcast_to(block_of, (mb, LANES)), var_found, 0.0),
            axis=0,
            keepdims=True,
        )
        for parity in range(2):
            d = 2 * q + parity

            @pl.when(d != a)
            def _():
                pltpu.make_async_remote_copy(
                    src_ref=zs.at[d],
                    dst_ref=zr.at[a],
                    send_sem=z_send,
                    recv_sem=z_recv,
                    device_id=(d, s),
                    device_id_type=MESH,
                ).start()
                pltpu.make_async_remote_copy(
                    src_ref=vs.at[q],
                    dst_ref=vr.at[a],
                    send_sem=v_send,
                    recv_sem=v_recv,
                    device_id=(d, s),
                    device_id_type=MESH,
                ).start()

            @pl.when(d == a)
            def _():
                pltpu.make_async_copy(zs.at[d], zr.at[a], z_recv).start()
                pltpu.make_async_copy(vs.at[q], vr.at[a], v_recv).start()

        return carry

    lax.fori_loop(0, chunks, route_out, 0)

    sub_q = lax.broadcasted_iota(i32, (mb, LANES), 0)
    lane_q = lax.broadcasted_iota(i32, (mb, LANES), 1)
    sub_l = lax.broadcasted_iota(i32, (LANES, LANES), 0)

    def invert(q, total):
        where_at = table_row(1, q)
        mine = jnp.broadcast_to(lax.shift_right_arithmetic(where_at, 7), (mb, LANES)) == sub_q
        left = jnp.concatenate(
            [jnp.where(mine, lane_q, 0).astype(f32), jnp.where(mine, q, 0).astype(f32)], axis=0
        ).astype(bf16)
        hit = jnp.broadcast_to(where_at & (LANES - 1), (LANES, LANES)) == sub_l
        right = jnp.where(hit, 1.0, 0.0).astype(bf16)
        return total + lax.dot_general(left, right, NT, preferred_element_type=f32)

    inverse = lax.fori_loop(0, chunks, invert, jnp.zeros((2 * mb, LANES), f32))
    inv_lane[...] = inverse[:mb].astype(i32) & (LANES - 1)
    inv_q[...] = inverse[mb:].astype(i32)

    def index_tiles(n, carry):
        for j in range(mb):
            which = all_tiles
            for k in range(touched):
                tile = j * touched + k
                which = jnp.where(pos_ref[j, k] == n, tile, which)
            tile_index[n, j] = which
        return carry

    lax.fori_loop(0, slots, index_tiles, 0)
    tiles[all_tiles] = jnp.zeros((LANES, LANES), bf16)

    gain_copy.wait()
    gain_t[...] = gain[...].T
    tiles_copy.wait()

    def predict(step):
        frontier_wait(step)

        def body(j, carry):
            total = jnp.zeros((snaps, LANES), f32)
            for k in range(touched):
                total += lax.dot_general(
                    aug[pos_ref[j, k]],
                    tiles[j * touched + k],
                    NT,
                    preferred_element_type=f32,
                )
            resid[j] = total
            return carry

        lax.fori_loop(0, mb, body, 0, unroll=2)

    predict(0)

    pltpu.make_async_copy(zr, zr, z_recv).wait()
    pltpu.make_async_copy(vr, vr, v_recv).wait()

    def unpack(q, carry):
        even, odd = zr[2 * q], zr[2 * q + 1]
        arrived[q, pl.ds(0, half)] = jnp.where(lane_h < cap, even, pltpu.roll(odd, cap, 1))
        arrived[q, pl.ds(half, half)] = jnp.where(lane_h < cap, pltpu.roll(even, cap, 1), odd)
        return carry

    lax.fori_loop(0, chunks, unpack, 0, unroll=2)
    variances = jnp.concatenate([vr[c] for c in range(areas)], axis=0)
    sub_a = lax.broadcasted_iota(i32, (areas, LANES), 0)
    my_half = lax.rem(a, 2) * cap

    def reorder(j, carry):
        lane_of = inv_lane[pl.ds(j, 1), :]
        chunk_of = inv_q[pl.ds(j, 1), :]
        lanes = jnp.broadcast_to(lane_of, (snaps, LANES))
        from_chunk = jnp.broadcast_to(chunk_of, (snaps, LANES))
        taken = jnp.zeros((snaps, LANES), f32)
        for q in range(chunks):
            found = jnp.take_along_axis(arrived[q], lanes, axis=1)
            taken = jnp.where(from_chunk == q, found, taken)
        z_own[j] = taken
        hub = 2 * chunk_of + lax.shift_right_arithmetic(lane_of, 6)
        lane_v = (lane_of & (cap - 1)) + my_half
        found = jnp.take_along_axis(
            variances, jnp.broadcast_to(lane_v, (areas, LANES)), axis=1
        )
        v_own[pl.ds(j, 1), :] = jnp.sum(
            jnp.where(jnp.broadcast_to(hub, (areas, LANES)) == sub_a, found, 0.0),
            axis=0,
            keepdims=True,
        )
        return carry

    lax.fori_loop(0, mb, reorder, 0)

    def spread_copy(step, i):
        peer = lax.rem(s + i, peers)
        return pltpu.make_async_remote_copy(
            src_ref=ssr.at[step, s],
            dst_ref=ssr.at[step, s],
            send_sem=s_send.at[step, i],
            recv_sem=s_recv.at[step, s],
            device_id=(a, peer),
            device_id_type=MESH,
        )

    def spread_wait(step, i):
        source = lax.rem(s + i, peers)
        pltpu.make_async_remote_copy(
            src_ref=ssr.at[step, source],
            dst_ref=ssr.at[step, source],
            send_sem=s_send.at[step, i],
            recv_sem=s_recv.at[step, source],
            device_id=(a, source),
            device_id_type=MESH,
        ).wait_recv()

    def boundary_copy(step, side):
        return pltpu.make_async_remote_copy(
            src_ref=bs.at[step, side],
            dst_ref=br.at[step, 1 - side, pl.ds(0, ties)],
            send_sem=b_send.at[step, side],
            recv_sem=b_recv.at[step, side],
            device_id=(a - 1 if side == 0 else a + 1, s),
            device_id_type=MESH,
        )

    def ring_copy(step, way, hop, piece, chunk):
        beside = lax.rem(s + 1, peers) if way == 0 else lax.rem(s + peers - 1, peers)
        part = pl.ds(piece * piece_units, piece_units)
        return pltpu.make_async_remote_copy(
            src_ref=gath.at[step, chunk, part],
            dst_ref=gath.at[step, chunk, part],
            send_sem=ring_send.at[step, way, hop - 1, piece],
            recv_sem=ring_recv.at[step, way, hop - 1, piece],
            device_id=(a, beside),
            device_id_type=MESH,
        )

    def ring_pieces(way, hop):
        if hop < reach:
            return range(pieces)
        return range(pieces // 2) if way == 0 else range(pieces // 2, pieces)

    def came_from(way, hop):
        return lax.rem(s + peers - hop, peers) if way == 0 else lax.rem(s + hop, peers)

    def update_copy(step, chunk):
        return pltpu.make_async_remote_copy(
            src_ref=us.at[step, chunk],
            dst_ref=ur.at[step, s],
            send_sem=u_send.at[step, chunk],
            recv_sem=u_recv.at[step, s],
            device_id=(a, chunk),
            device_id_type=MESH,
        )

    def slot_pair(n2):
        total = jnp.zeros((snaps, 2 * LANES), f32)
        for jp in range(mb // 2):
            left = [tiles[tile_index[2 * n2, 2 * jp + r]] for r in range(2)]
            right = [tiles[tile_index[2 * n2 + 1, 2 * jp + r]] for r in range(2)]
            weights = jnp.concatenate(
                [jnp.concatenate(left, axis=0), jnp.concatenate(right, axis=0)], axis=1
            )
            total += jnp.dot(wgt[jp], weights, preferred_element_type=f32)
        return total

    def gain_piece(step, chunk, piece):
        total = jnp.zeros((snaps, rows), f32)
        for u in range(piece * piece_units, (piece + 1) * piece_units):
            total += jnp.dot(
                gath[step, chunk, u],
                gain_t[u * 2 * LANES : (u + 1) * 2 * LANES, :],
                preferred_element_type=f32,
            )
        return total

    for step in range(ITERS):
        if step > 0:
            frontier_start(step)
            predict(step)

        for j in range(mb):
            left_over = z_own[j] - resid[j]
            resid[j] = left_over
            ssr[step, s, pl.ds(j, 1), :] = jnp.sum(
                left_over * left_over, axis=0, keepdims=True
            )
        for i in range(1, peers):
            spread_copy(step, i).start()
        for i in range(1, peers):
            spread_wait(step, i)
        total = ssr[step, 0]
        for i in range(1, peers):
            total += ssr[step, i]
        scale = v_own[...] + total / snaps_all
        for j in range(mb):
            wgt[j // 2, :, (j % 2) * LANES : (j % 2 + 1) * LANES] = (
                resid[j] / scale[j : j + 1, :]
            ).astype(bf16)

        def outer_slots(i, carry):
            pair = slot_pair(nb // 2 + i)
            side, first = lax.div(i, ties // 2), lax.rem(i, ties // 2) * 2
            bs[step, side, first] = pair[:, :LANES]
            bs[step, side, first + 1] = pair[:, LANES:]
            return carry

        lax.fori_loop(0, ties, outer_slots, 0)

        @pl.when(has_lower)
        def _():
            boundary_copy(step, 0).start()

        @pl.when(has_upper)
        def _():
            boundary_copy(step, 1).start()

        def own_slots(n2, carry):
            pair = slot_pair(n2)
            grads[2 * n2] = pair[:, :LANES]
            grads[2 * n2 + 1] = pair[:, LANES:]
            return carry

        lax.fori_loop(0, nb // 2, own_slots, 0)

        @pl.when(has_upper)
        def _():
            boundary_copy(step, 0).wait_recv()

        @pl.when(has_lower)
        def _():
            boundary_copy(step, 1).wait_recv()

        for block in range(nb):
            total = grads[block]
            for side in range(2):
                which = ties
                for t in range(ties):
                    which = jnp.where(ties_ref[side, t] == block, t, which)
                total += br[step, side, which]
            gath[step, s, block // 2, :, (block % 2) * LANES : (block % 2 + 1) * LANES] = (
                total.astype(bf16)
            )
            if block % (2 * piece_units) == 2 * piece_units - 1:
                for way in range(2):
                    ring_copy(step, way, 1, block // (2 * piece_units), s).start()

        own = gain_piece(step, s, 0)
        for piece in range(1, pieces):
            own += gain_piece(step, s, piece)
        ur[step, s] = own

        for hop in range(1, reach + 1):
            sums = [None, None]
            for turn in range(len(ring_pieces(0, hop))):
                for way in range(2):
                    piece = ring_pieces(way, hop)[turn]
                    chunk = came_from(way, hop)
                    ring_copy(step, way, hop, piece, chunk).wait_recv()
                    if hop < reach and piece in ring_pieces(way, hop + 1):
                        ring_copy(step, way, hop + 1, piece, chunk).start()
                for way in range(2):
                    piece = ring_pieces(way, hop)[turn]
                    part = gain_piece(step, came_from(way, hop), piece)
                    sums[way] = part if sums[way] is None else sums[way] + part
            if hop < reach:
                for way in range(2):
                    us[step, came_from(way, hop)] = sums[way]
                    update_copy(step, came_from(way, hop)).start()
            else:
                us[step, came_from(0, hop)] = sums[0] + sums[1]
                update_copy(step, came_from(0, hop)).start()

        before = x_ref if step == 0 else out_ref
        for i in range(peers):

            @pl.when(i != s)
            def _():
                pltpu.make_async_remote_copy(
                    src_ref=us.at[step, i],
                    dst_ref=ur.at[step, i],
                    send_sem=u_send.at[step, i],
                    recv_sem=u_recv.at[step, i],
                    device_id=(a, i),
                    device_id_type=MESH,
                ).wait_recv()

        for i in range(peers):
            cols = slice(i * rows, (i + 1) * rows)
            after = before[:, cols] + ur[step, i]
            out_ref[:, cols] = after
            if step + 1 < ITERS:
                for r in range(rows // LANES):
                    aug[i * (rows // LANES) + r] = after[
                        :, r * LANES : (r + 1) * LANES
                    ].astype(bf16)

    pltpu.make_async_copy(
        zs.at[pl.ds(0, areas - 1)], zr.at[pl.ds(0, areas - 1)], z_send
    ).wait()
    pltpu.make_async_copy(
        vr.at[pl.ds(0, areas - 1)], vr.at[pl.ds(0, areas - 1)], v_send
    ).wait()
    for step in range(ITERS):

        @pl.when(has_lower)
        def _():
            frontier_copy(step, 0).wait_send()
            boundary_copy(step, 0).wait_send()

        @pl.when(has_upper)
        def _():
            frontier_copy(step, 1).wait_send()
            boundary_copy(step, 1).wait_send()

        for i in range(1, peers):
            spread_copy(step, i).wait_send()
            update_copy(step, lax.rem(s + i, peers)).wait_send()
        for way in range(2):
            for hop in range(1, reach + 1):
                for piece in ring_pieces(way, hop):
                    ring_copy(step, way, hop, piece, s).wait_send()


def on_device(
    phasor_readings,
    reading_error_spread,
    starting_voltages,
    derivative_pieces,
    derivative_tile_position,
    frontier_voltage_pieces,
    holder_line_order,
    hub_line_order,
    reciprocal_normal_operator,
):
    areas, peers = lax.axis_size("area"), lax.axis_size("snap")
    snaps, states = starting_voltages.shape
    nb = states // LANES
    mb, touched = derivative_tile_position.shape[1:]
    ties = frontier_voltage_pieces.shape[2]
    cap = holder_line_order.shape[2]
    rows = states // peers
    chunks = areas * cap // LANES
    slots = nb + 2 * ties
    all_tiles = mb * touched
    units = nb // 2
    reach = peers // 2
    pieces = units // 2
    f32, bf16, i32 = jnp.float32, jnp.bfloat16, jnp.int32
    vmem = pl.BlockSpec(memory_space=pltpu.VMEM)
    smem = pl.BlockSpec(memory_space=pltpu.SMEM)
    hbm = pl.BlockSpec(memory_space=pltpu.HBM)
    dma = pltpu.SemaphoreType.DMA
    dims = (areas, peers, snaps, nb, mb, touched, ties, cap)
    return pl.pallas_call(
        functools.partial(step_kernel, dims),
        out_shape=jax.ShapeDtypeStruct((snaps, states), f32),
        in_specs=[vmem, vmem, vmem, hbm, smem, smem, vmem, vmem, hbm],
        out_specs=vmem,
        scratch_shapes=[
            pltpu.VMEM((all_tiles + 1, LANES, LANES), bf16),
            pltpu.VMEM((rows, states), bf16),
            pltpu.VMEM((states, rows), bf16),
            pltpu.SMEM((slots, mb), i32),
            pltpu.VMEM((2, areas, LANES), i32),
            pltpu.VMEM((areas, snaps // 2, LANES), f32),
            pltpu.VMEM((areas, snaps // 2, LANES), f32),
            pltpu.VMEM((chunks, 1, LANES), f32),
            pltpu.VMEM((areas, 1, LANES), f32),
            pltpu.VMEM((chunks, snaps, LANES), f32),
            pltpu.VMEM((mb, LANES), i32),
            pltpu.VMEM((mb, LANES), i32),
            pltpu.VMEM((mb, snaps, LANES), f32),
            pltpu.VMEM((mb, LANES), f32),
            pltpu.VMEM((slots + 1, snaps, LANES), bf16),
            pltpu.VMEM((ITERS, 2, ties, snaps, LANES), bf16),
            pltpu.VMEM((ITERS, 2, ties, snaps, LANES), bf16),
            pltpu.VMEM((mb, snaps, LANES), f32),
            pltpu.VMEM((ITERS, peers, mb, LANES), f32),
            pltpu.VMEM((mb // 2, snaps, 2 * LANES), bf16),
            pltpu.VMEM((nb, snaps, LANES), f32),
            pltpu.VMEM((ITERS, 2, ties, snaps, LANES), f32),
            pltpu.VMEM((ITERS, 2, ties + 1, snaps, LANES), f32),
            pltpu.VMEM((ITERS, peers, units, snaps, 2 * LANES), bf16),
            pltpu.VMEM((ITERS, peers, snaps, rows), f32),
            pltpu.VMEM((ITERS, peers, snaps, rows), f32),
            dma((2,)),
            dma(()),
            dma(()),
            dma(()),
            dma(()),
            dma((ITERS, 2)),
            dma((ITERS, 2)),
            dma((ITERS, peers)),
            dma((ITERS, peers)),
            dma((ITERS, 2)),
            dma((ITERS, 2)),
            dma((ITERS, 2, reach, pieces)),
            dma((ITERS, 2, reach, pieces)),
            dma((ITERS, peers)),
            dma((ITERS, peers)),
        ],
        compiler_params=pltpu.CompilerParams(collective_id=0, has_side_effects=True),
        name="estimate",
    )(
        phasor_readings,
        reading_error_spread.reshape(mb, LANES),
        starting_voltages,
        derivative_pieces.reshape(all_tiles, LANES, LANES),
        derivative_tile_position[0],
        frontier_voltage_pieces[0],
        holder_line_order[0],
        hub_line_order[0],
        reciprocal_normal_operator,
    )


def solution(mesh):
    placed = (
        P("snap", "area"),
        P("area"),
        P("snap", "area"),
        P("area", None, None, None),
        P("area", None, None),
        P("area", None, None),
        P("area", None, None),
        P("area", None, None),
        P(("area", "snap"), None),
    )
    return jax.shard_map(
        on_device, mesh=mesh, in_specs=placed, out_specs=P("snap", "area"), check_vma=False
    )
```

```python
import functools

import jax
import jax.numpy as jnp
from jax import lax
from jax.experimental import pallas as pl
from jax.experimental.pallas import tpu as pltpu
from jax.sharding import PartitionSpec as P

ITERS = 2
UNROLL = (8, 8, 4, 4, 4)
LANES = 128
MESH = pl.DeviceIdType.MESH
NT = (((1,), (1,)), ((), ()))


def step_kernel(
    dims,
    z_ref,
    var_ref,
    x_ref,
    tiles_hbm,
    pos_ref,
    ties_ref,
    holder_ref,
    hub_ref,
    gain_hbm,
    out_ref,
    tiles,
    gain,
    gain_t,
    tile_index,
    table,
    zs,
    zr,
    vs,
    vr,
    arrived,
    inv_q,
    inv_lane,
    z_own,
    v_own,
    aug,
    fs,
    fr,
    resid,
    ssr,
    wgt,
    grads,
    bs,
    br,
    gath,
    us,
    ur,
    local_sem,
    z_send,
    z_recv,
    v_send,
    v_recv,
    f_send,
    f_recv,
    s_send,
    s_recv,
    b_send,
    b_recv,
    ring_send,
    ring_recv,
    u_send,
    u_recv,
):
    areas, peers, snaps, nb, mb, touched, ties, cap = dims
    half = snaps // 2
    chunks = areas * cap // LANES
    rows = nb * LANES // peers
    units = nb // 2
    piece_units = 2
    pieces = units // piece_units
    reach = peers // 2
    slots = nb + 2 * ties
    all_tiles = mb * touched
    snaps_all = snaps * peers
    f32, bf16, i32 = jnp.float32, jnp.bfloat16, jnp.int32

    a = lax.axis_index("area")
    s = lax.axis_index("snap")
    has_lower = a > 0
    has_upper = a < areas - 1

    tiles_copy = pltpu.make_async_copy(
        tiles_hbm, tiles.at[pl.ds(0, all_tiles)], local_sem.at[0]
    )
    gain_copy = pltpu.make_async_copy(gain_hbm, gain, local_sem.at[1])
    tiles_copy.start()
    gain_copy.start()

    barrier = pltpu.get_barrier_semaphore()

    def greet_area(i, carry):
        pl.semaphore_signal(
            barrier, inc=1, device_id=(lax.rem(a + i, areas), s), device_id_type=MESH
        )
        return carry

    def greet_snap(i, carry):
        pl.semaphore_signal(
            barrier, inc=1, device_id=(a, lax.rem(s + i, peers)), device_id_type=MESH
        )
        return carry

    lax.fori_loop(1, areas, greet_area, 0)
    lax.fori_loop(1, peers, greet_snap, 0)

    lane_a = lax.broadcasted_iota(i32, (areas, LANES), 1)
    for index, listing in enumerate((hub_ref, holder_ref)):
        both = jnp.concatenate([listing[...], listing[...]], axis=1)
        table[index] = both
    for block in range(nb):
        aug[block] = x_ref[:, block * LANES : (block + 1) * LANES].astype(bf16)
    aug[slots] = jnp.zeros((snaps, LANES), bf16)
    for step in range(ITERS):
        for side in range(2):
            br[step, side, ties] = jnp.zeros((snaps, LANES), f32)

    @pl.when(jnp.logical_not(has_lower))
    def _():
        for t in range(ties):
            aug[nb + t] = jnp.zeros((snaps, LANES), bf16)
            for step in range(ITERS):
                br[step, 0, t] = jnp.zeros((snaps, LANES), f32)

    @pl.when(jnp.logical_not(has_upper))
    def _():
        for t in range(ties):
            aug[nb + ties + t] = jnp.zeros((snaps, LANES), bf16)
            for step in range(ITERS):
                br[step, 1, t] = jnp.zeros((snaps, LANES), f32)

    pl.semaphore_wait(barrier, areas - 1 + peers - 1)

    def frontier_copy(step, side):
        return pltpu.make_async_remote_copy(
            src_ref=fs.at[step, side],
            dst_ref=fr.at[step, 1 - side],
            send_sem=f_send.at[step, side],
            recv_sem=f_recv.at[step, side],
            device_id=(a - 1 if side == 0 else a + 1, s),
            device_id_type=MESH,
        )

    def frontier_start(step):
        for side in range(2):
            for t in range(ties):
                entry = ties_ref[side, t]
                fs[step, side, t] = aug[jnp.where(entry >= 0, entry, slots)]

        @pl.when(has_lower)
        def _():
            frontier_copy(step, 0).start()

        @pl.when(has_upper)
        def _():
            frontier_copy(step, 1).start()

    def frontier_wait(step):
        @pl.when(has_lower)
        def _():
            frontier_copy(step, 1).wait_recv()
            for t in range(ties):
                aug[nb + t] = fr[step, 0, t]

        @pl.when(has_upper)
        def _():
            frontier_copy(step, 0).wait_recv()
            for t in range(ties):
                aug[nb + ties + t] = fr[step, 1, t]

    frontier_start(0)

    def table_row(index, q):
        even = table[index, pl.ds(2 * q, 1), :]
        odd = table[index, pl.ds(2 * q + 1, 1), :]
        lane = lax.broadcasted_iota(i32, (1, LANES), 1)
        return jnp.where(lane < cap, even, odd)

    lane_h = lax.broadcasted_iota(i32, (half, LANES), 1)

    wide = min(chunks, 4)
    tall = chunks // wide

    def route_out(i, carry):
        k = lax.rem(i, tall)
        turn = (k + 1) // 2
        dy = tall // 2 + turn * (1 - 2 * (k % 2))
        dx = lax.rem(wide // 2 + lax.div(i, tall), wide)
        chip = lax.div(a, 2)
        q = lax.rem(lax.div(chip, wide) + dy, tall) * wide + lax.rem(lax.rem(chip, wide) + dx, wide)
        where_at = table_row(0, q)
        block_of = lax.shift_right_arithmetic(where_at, 7)
        lane_of = where_at & (LANES - 1)
        lanes = jnp.broadcast_to(lane_of, (snaps, LANES))
        from_block = jnp.broadcast_to(block_of, (snaps, LANES))
        taken = jnp.zeros((snaps, LANES), f32)
        for block in range(mb):
            found = jnp.take_along_axis(
                z_ref[:, block * LANES : (block + 1) * LANES], lanes, axis=1
            )
            taken = jnp.where(from_block == block, found, taken)
        low, high = taken[:half], taken[half:]
        zs[2 * q] = jnp.where(lane_h < cap, low, pltpu.roll(high, cap, 1))
        zs[2 * q + 1] = jnp.where(lane_h < cap, pltpu.roll(low, cap, 1), high)
        var_found = jnp.take_along_axis(
            var_ref[...], jnp.broadcast_to(lane_of, (mb, LANES)), axis=1
        )
        var_rows = lax.broadcasted_iota(i32, (mb, LANES), 0)
        vs[q] = jnp.sum(
            jnp.where(var_rows == jnp.broadcast_to(block_of, (mb, LANES)), var_found, 0.0),
            axis=0,
            keepdims=True,
        )
        for parity in range(2):
            d = 2 * q + parity

            @pl.when(d != a)
            def _():
                pltpu.make_async_remote_copy(
                    src_ref=zs.at[d],
                    dst_ref=zr.at[a],
                    send_sem=z_send,
                    recv_sem=z_recv,
                    device_id=(d, s),
                    device_id_type=MESH,
                ).start()
                pltpu.make_async_remote_copy(
                    src_ref=vs.at[q],
                    dst_ref=vr.at[a],
                    send_sem=v_send,
                    recv_sem=v_recv,
                    device_id=(d, s),
                    device_id_type=MESH,
                ).start()

            @pl.when(d == a)
            def _():
                pltpu.make_async_copy(zs.at[d], zr.at[a], z_recv).start()
                pltpu.make_async_copy(vs.at[q], vr.at[a], v_recv).start()

        return carry

    lax.fori_loop(0, chunks, route_out, 0, unroll=UNROLL[2])

    sub_q = lax.broadcasted_iota(i32, (mb, LANES), 0)
    lane_q = lax.broadcasted_iota(i32, (mb, LANES), 1)
    sub_l = lax.broadcasted_iota(i32, (LANES, LANES), 0)

    def invert(q, total):
        where_at = table_row(1, q)
        mine = jnp.broadcast_to(lax.shift_right_arithmetic(where_at, 7), (mb, LANES)) == sub_q
        left = jnp.concatenate(
            [jnp.where(mine, lane_q, 0).astype(f32), jnp.where(mine, q, 0).astype(f32)], axis=0
        ).astype(bf16)
        hit = jnp.broadcast_to(where_at & (LANES - 1), (LANES, LANES)) == sub_l
        right = jnp.where(hit, 1.0, 0.0).astype(bf16)
        return total + lax.dot_general(left, right, NT, preferred_element_type=f32)

    inverse = lax.fori_loop(
        0, chunks, invert, jnp.zeros((2 * mb, LANES), f32), unroll=UNROLL[0]
    )
    inv_lane[...] = inverse[:mb].astype(i32) & (LANES - 1)
    inv_q[...] = inverse[mb:].astype(i32)

    def index_tiles(n, carry):
        for j in range(mb):
            which = all_tiles
            for k in range(touched):
                tile = j * touched + k
                which = jnp.where(pos_ref[k, j] == n, tile, which)
            tile_index[n, j] = which
        return carry

    tiles_copy.wait()

    def predict(step):
        frontier_wait(step)

        def body(j, carry):
            total = jnp.zeros((snaps, LANES), f32)
            for k in range(touched):
                total += lax.dot_general(
                    aug[pos_ref[k, j]],
                    tiles[j * touched + k],
                    NT,
                    preferred_element_type=f32,
                )
            resid[j] = total
            return carry

        lax.fori_loop(0, mb, body, 0, unroll=min(mb, UNROLL[1]))

    predict(0)

    pltpu.make_async_copy(zr, zr, z_recv).wait()
    pltpu.make_async_copy(vr, vr, v_recv).wait()

    def unpack(q, carry):
        even, odd = zr[2 * q], zr[2 * q + 1]
        arrived[q, pl.ds(0, half)] = jnp.where(lane_h < cap, even, pltpu.roll(odd, cap, 1))
        arrived[q, pl.ds(half, half)] = jnp.where(lane_h < cap, pltpu.roll(even, cap, 1), odd)
        return carry

    lax.fori_loop(0, chunks, unpack, 0, unroll=4)
    variances = jnp.concatenate([vr[c] for c in range(areas)], axis=0)
    sub_a = lax.broadcasted_iota(i32, (areas, LANES), 0)
    my_half = lax.rem(a, 2) * cap

    def reorder(j, carry):
        lane_of = inv_lane[pl.ds(j, 1), :]
        chunk_of = inv_q[pl.ds(j, 1), :]
        lanes = jnp.broadcast_to(lane_of, (snaps, LANES))
        from_chunk = jnp.broadcast_to(chunk_of, (snaps, LANES))
        taken = jnp.zeros((snaps, LANES), f32)
        for q in range(chunks):
            found = jnp.take_along_axis(arrived[q], lanes, axis=1)
            taken = jnp.where(from_chunk == q, found, taken)
        z_own[j] = taken
        hub = 2 * chunk_of + lax.shift_right_arithmetic(lane_of, 6)
        lane_v = (lane_of & (cap - 1)) + my_half
        found = jnp.take_along_axis(
            variances, jnp.broadcast_to(lane_v, (areas, LANES)), axis=1
        )
        v_own[pl.ds(j, 1), :] = jnp.sum(
            jnp.where(jnp.broadcast_to(hub, (areas, LANES)) == sub_a, found, 0.0),
            axis=0,
            keepdims=True,
        )
        return carry

    lax.fori_loop(0, mb, reorder, 0, unroll=min(mb, UNROLL[3]))

    def spread_copy(step, i):
        peer = lax.rem(s + i, peers)
        return pltpu.make_async_remote_copy(
            src_ref=ssr.at[step, s],
            dst_ref=ssr.at[step, s],
            send_sem=s_send.at[step, i],
            recv_sem=s_recv.at[step, s],
            device_id=(a, peer),
            device_id_type=MESH,
        )

    def spread_wait(step, i):
        source = lax.rem(s + i, peers)
        pltpu.make_async_remote_copy(
            src_ref=ssr.at[step, source],
            dst_ref=ssr.at[step, source],
            send_sem=s_send.at[step, i],
            recv_sem=s_recv.at[step, source],
            device_id=(a, source),
            device_id_type=MESH,
        ).wait_recv()

    def boundary_copy(step, side, part):
        return pltpu.make_async_remote_copy(
            src_ref=bs.at[step, side, pl.ds(2 * part, 2)],
            dst_ref=br.at[step, 1 - side, pl.ds(2 * part, 2)],
            send_sem=b_send.at[step, side, part],
            recv_sem=b_recv.at[step, side, part],
            device_id=(a - 1 if side == 0 else a + 1, s),
            device_id_type=MESH,
        )

    def ring_copy(step, way, hop, piece, chunk):
        beside = lax.rem(s + 1, peers) if way == 0 else lax.rem(s + peers - 1, peers)
        part = pl.ds(piece * piece_units, piece_units)
        return pltpu.make_async_remote_copy(
            src_ref=gath.at[step, chunk, part],
            dst_ref=gath.at[step, chunk, part],
            send_sem=ring_send.at[step, way, hop - 1, piece],
            recv_sem=ring_recv.at[step, way, hop - 1, piece],
            device_id=(a, beside),
            device_id_type=MESH,
        )

    def ring_pieces(way, hop):
        if hop < reach:
            return range(pieces)
        return range(pieces // 2) if way == 0 else range(pieces // 2, pieces)

    def came_from(way, hop):
        return lax.rem(s + peers - hop, peers) if way == 0 else lax.rem(s + hop, peers)

    def update_copy(step, chunk):
        return pltpu.make_async_remote_copy(
            src_ref=us.at[step, chunk],
            dst_ref=ur.at[step, s],
            send_sem=u_send.at[step, chunk],
            recv_sem=u_recv.at[step, s],
            device_id=(a, chunk),
            device_id_type=MESH,
        )

    def slot_pair(n2):
        total = jnp.zeros((snaps, 2 * LANES), f32)
        for jp in range(mb // 2):
            left = [tiles[tile_index[2 * n2, 2 * jp + r]] for r in range(2)]
            right = [tiles[tile_index[2 * n2 + 1, 2 * jp + r]] for r in range(2)]
            weights = jnp.concatenate(
                [jnp.concatenate(left, axis=0), jnp.concatenate(right, axis=0)], axis=1
            )
            total += jnp.dot(wgt[jp], weights, preferred_element_type=f32)
        return total

    def gain_piece(step, chunk, piece):
        total = jnp.zeros((snaps, rows), f32)
        for u in range(piece * piece_units, (piece + 1) * piece_units):
            total += jnp.dot(
                gath[step, chunk, u],
                gain_t[u * 2 * LANES : (u + 1) * 2 * LANES, :],
                preferred_element_type=f32,
            )
        return total

    for step in range(ITERS):
        if step > 0:
            frontier_start(step)
            predict(step)

        for j in range(mb):
            left_over = z_own[j] - resid[j]
            resid[j] = left_over
            ssr[step, s, pl.ds(j, 1), :] = jnp.sum(
                left_over * left_over, axis=0, keepdims=True
            )
        for i in range(1, peers):
            spread_copy(step, i).start()
        if step == 0:
            lax.fori_loop(0, slots, index_tiles, 0)
            tiles[all_tiles] = jnp.zeros((LANES, LANES), bf16)
            gain_copy.wait()
            gain_t[...] = gain[...].T
        for i in range(1, peers):
            spread_wait(step, i)
        total = ssr[step, 0]
        for i in range(1, peers):
            total += ssr[step, i]
        scale = v_own[...] + total / snaps_all
        for j in range(mb):
            wgt[j // 2, :, (j % 2) * LANES : (j % 2 + 1) * LANES] = (
                resid[j] / scale[j : j + 1, :]
            ).astype(bf16)

        for side in range(2):
            for part in range(ties // 2):
                pair = slot_pair(nb // 2 + side * (ties // 2) + part)
                bs[step, side, 2 * part] = pair[:, :LANES]
                bs[step, side, 2 * part + 1] = pair[:, LANES:]

                @pl.when(has_lower if side == 0 else has_upper)
                def _():
                    boundary_copy(step, side, part).start()

        def own_slots(n2, carry):
            pair = slot_pair(n2)
            grads[2 * n2] = pair[:, :LANES]
            grads[2 * n2 + 1] = pair[:, LANES:]
            return carry

        lax.fori_loop(0, nb // 2, own_slots, 0, unroll=min(nb // 2, UNROLL[4]))

        @pl.when(has_upper)
        def _():
            for part in range(ties // 2):
                boundary_copy(step, 0, part).wait_recv()

        @pl.when(has_lower)
        def _():
            for part in range(ties // 2):
                boundary_copy(step, 1, part).wait_recv()

        for block in range(nb):
            total = grads[block]
            for side in range(2):
                which = ties
                for t in range(ties):
                    which = jnp.where(ties_ref[side, t] == block, t, which)
                total += br[step, side, which]
            gath[step, s, block // 2, :, (block % 2) * LANES : (block % 2 + 1) * LANES] = (
                total.astype(bf16)
            )
            if block % (2 * piece_units) == 2 * piece_units - 1:
                for way in range(2):
                    ring_copy(step, way, 1, block // (2 * piece_units), s).start()

        own = gain_piece(step, s, 0)
        for piece in range(1, pieces):
            own += gain_piece(step, s, piece)
        ur[step, s] = own.astype(bf16)

        for hop in range(1, reach + 1):
            sums = [None, None]
            for turn in range(len(ring_pieces(0, hop))):
                for way in range(2):
                    piece = ring_pieces(way, hop)[turn]
                    chunk = came_from(way, hop)
                    ring_copy(step, way, hop, piece, chunk).wait_recv()
                    if hop < reach and piece in ring_pieces(way, hop + 1):
                        ring_copy(step, way, hop + 1, piece, chunk).start()
                for way in range(2):
                    piece = ring_pieces(way, hop)[turn]
                    part = gain_piece(step, came_from(way, hop), piece)
                    sums[way] = part if sums[way] is None else sums[way] + part
            if hop < reach:
                for way in range(2):
                    us[step, came_from(way, hop)] = sums[way].astype(bf16)
                    update_copy(step, came_from(way, hop)).start()
            else:
                us[step, came_from(0, hop)] = (sums[0] + sums[1]).astype(bf16)
                update_copy(step, came_from(0, hop)).start()

        before = x_ref if step == 0 else out_ref
        for i in range(peers):

            @pl.when(i != s)
            def _():
                pltpu.make_async_remote_copy(
                    src_ref=us.at[step, i],
                    dst_ref=ur.at[step, i],
                    send_sem=u_send.at[step, i],
                    recv_sem=u_recv.at[step, i],
                    device_id=(a, i),
                    device_id_type=MESH,
                ).wait_recv()

        for i in range(peers):
            cols = slice(i * rows, (i + 1) * rows)
            after = before[:, cols] + ur[step, i].astype(f32)
            out_ref[:, cols] = after
            if step + 1 < ITERS:
                for r in range(rows // LANES):
                    aug[i * (rows // LANES) + r] = after[
                        :, r * LANES : (r + 1) * LANES
                    ].astype(bf16)

    pltpu.make_async_copy(
        zs.at[pl.ds(0, areas - 1)], zr.at[pl.ds(0, areas - 1)], z_send
    ).wait()
    pltpu.make_async_copy(
        vr.at[pl.ds(0, areas - 1)], vr.at[pl.ds(0, areas - 1)], v_send
    ).wait()
    for step in range(ITERS):

        @pl.when(has_lower)
        def _():
            frontier_copy(step, 0).wait_send()
            for part in range(ties // 2):
                boundary_copy(step, 0, part).wait_send()

        @pl.when(has_upper)
        def _():
            frontier_copy(step, 1).wait_send()
            for part in range(ties // 2):
                boundary_copy(step, 1, part).wait_send()

        for i in range(1, peers):
            spread_copy(step, i).wait_send()
            update_copy(step, lax.rem(s + i, peers)).wait_send()
        for way in range(2):
            for hop in range(1, reach + 1):
                for piece in ring_pieces(way, hop):
                    ring_copy(step, way, hop, piece, s).wait_send()


def on_device(
    phasor_readings,
    reading_error_spread,
    starting_voltages,
    derivative_pieces,
    derivative_tile_position,
    frontier_voltage_pieces,
    holder_line_order,
    hub_line_order,
    reciprocal_normal_operator,
):
    areas, peers = lax.axis_size("area"), lax.axis_size("snap")
    snaps, states = starting_voltages.shape
    nb = states // LANES
    mb, touched = derivative_tile_position.shape[1:]
    ties = frontier_voltage_pieces.shape[2]
    cap = holder_line_order.shape[2]
    rows = states // peers
    chunks = areas * cap // LANES
    slots = nb + 2 * ties
    all_tiles = mb * touched
    units = nb // 2
    reach = peers // 2
    pieces = units // 2
    f32, bf16, i32 = jnp.float32, jnp.bfloat16, jnp.int32
    vmem = pl.BlockSpec(memory_space=pltpu.VMEM)
    smem = pl.BlockSpec(memory_space=pltpu.SMEM)
    hbm = pl.BlockSpec(memory_space=pltpu.HBM)
    dma = pltpu.SemaphoreType.DMA
    dims = (areas, peers, snaps, nb, mb, touched, ties, cap)
    return pl.pallas_call(
        functools.partial(step_kernel, dims),
        out_shape=jax.ShapeDtypeStruct((snaps, states), f32),
        in_specs=[vmem, vmem, vmem, hbm, smem, smem, vmem, vmem, hbm],
        out_specs=vmem,
        scratch_shapes=[
            pltpu.VMEM((all_tiles + 1, LANES, LANES), bf16),
            pltpu.VMEM((rows, states), bf16),
            pltpu.VMEM((states, rows), bf16),
            pltpu.SMEM((slots, mb), i32),
            pltpu.VMEM((2, areas, LANES), i32),
            pltpu.VMEM((areas, snaps // 2, LANES), f32),
            pltpu.VMEM((areas, snaps // 2, LANES), f32),
            pltpu.VMEM((chunks, 1, LANES), f32),
            pltpu.VMEM((areas, 1, LANES), f32),
            pltpu.VMEM((chunks, snaps, LANES), f32),
            pltpu.VMEM((mb, LANES), i32),
            pltpu.VMEM((mb, LANES), i32),
            pltpu.VMEM((mb, snaps, LANES), f32),
            pltpu.VMEM((mb, LANES), f32),
            pltpu.VMEM((slots + 1, snaps, LANES), bf16),
            pltpu.VMEM((ITERS, 2, ties, snaps, LANES), bf16),
            pltpu.VMEM((ITERS, 2, ties, snaps, LANES), bf16),
            pltpu.VMEM((mb, snaps, LANES), f32),
            pltpu.VMEM((ITERS, peers, mb, LANES), f32),
            pltpu.VMEM((mb // 2, snaps, 2 * LANES), bf16),
            pltpu.VMEM((nb, snaps, LANES), f32),
            pltpu.VMEM((ITERS, 2, ties, snaps, LANES), f32),
            pltpu.VMEM((ITERS, 2, ties + 1, snaps, LANES), f32),
            pltpu.VMEM((ITERS, peers, units, snaps, 2 * LANES), bf16),
            pltpu.VMEM((ITERS, peers, snaps, rows), bf16),
            pltpu.VMEM((ITERS, peers, snaps, rows), bf16),
            dma((2,)),
            dma(()),
            dma(()),
            dma(()),
            dma(()),
            dma((ITERS, 2)),
            dma((ITERS, 2)),
            dma((ITERS, peers)),
            dma((ITERS, peers)),
            dma((ITERS, 2, ties // 2)),
            dma((ITERS, 2, ties // 2)),
            dma((ITERS, 2, reach, pieces)),
            dma((ITERS, 2, reach, pieces)),
            dma((ITERS, peers)),
            dma((ITERS, peers)),
        ],
        compiler_params=pltpu.CompilerParams(collective_id=0, has_side_effects=True),
        name="estimate",
    )(
        phasor_readings,
        reading_error_spread.reshape(mb, LANES),
        starting_voltages,
        derivative_pieces.reshape(all_tiles, LANES, LANES),
        derivative_tile_position[0].T,
        frontier_voltage_pieces[0],
        holder_line_order[0],
        hub_line_order[0],
        reciprocal_normal_operator,
    )


def solution(mesh):
    placed = (
        P("snap", "area"),
        P("area"),
        P("snap", "area"),
        P("area", None, None, None),
        P("area", None, None),
        P("area", None, None),
        P("area", None, None),
        P("area", None, None),
        P(("area", "snap"), None),
    )
    return jax.shard_map(
        on_device, mesh=mesh, in_specs=placed, out_specs=P("snap", "area"), check_vma=False
    )
```

```python
import functools

import jax
import jax.numpy as jnp
from jax import lax
from jax.experimental import pallas as pl
from jax.experimental.pallas import tpu as pltpu
from jax.sharding import PartitionSpec as P

ITERS = 2
UNROLL = (8, 8, 4)
ARRIVALS = (
    (1, 0), (1, 1), (1, 2), (2, 0), (2, 1), (1, 3), (3, 0),
    (3, 1), (2, 2), (2, 3), (4, 0), (4, 1), (3, 2), (3, 3),
)
LANES = 128
MESH = pl.DeviceIdType.MESH
NT = (((1,), (1,)), ((), ()))


def step_kernel(
    dims,
    z_hbm,
    var_hbm,
    x_hbm,
    tiles_hbm,
    pos_hbm,
    ties_hbm,
    holder_hbm,
    hub_hbm,
    gain_hbm,
    out_ref,
    z_ref,
    var_ref,
    x_ref,
    pos_ref,
    ties_ref,
    holder_ref,
    hub_ref,
    load_sem,
    tiles,
    gain,
    gain_t,
    tile_index,
    table,
    zs,
    zr,
    vs,
    vr,
    arrived,
    inv_q,
    inv_lane,
    z_own,
    v_own,
    aug,
    fs,
    fr,
    resid,
    ssr,
    wgt,
    grads,
    bs,
    br,
    gath,
    us,
    ur,
    held,
    part_grad,
    local_sem,
    x_send,
    x_recv,
    z_send,
    z_recv,
    v_send,
    v_recv,
    f_send,
    f_recv,
    s_send,
    s_recv,
    b_send,
    b_recv,
    ring_send,
    ring_recv,
    u_send,
    u_recv,
):
    areas, peers, snaps, nb, mb, touched, ties, cap = dims
    half = snaps // 2
    chunks = areas * cap // LANES
    rows = nb * LANES // peers
    units = nb // 2
    piece_units = 2
    pieces = units // piece_units
    reach = peers // 2
    slots = nb + 2 * ties
    all_tiles = mb * touched
    snaps_all = snaps * peers
    f32, bf16, i32 = jnp.float32, jnp.bfloat16, jnp.int32

    a = lax.axis_index("area")
    s = lax.axis_index("snap")
    has_lower = a > 0
    has_upper = a < areas - 1

    tiles_copy = pltpu.make_async_copy(
        tiles_hbm, tiles, local_sem.at[0]
    )
    gain_copy = pltpu.make_async_copy(gain_hbm, gain, local_sem.at[1])
    loads = [
        pltpu.make_async_copy(source, target, load_sem.at[i])
        for i, (source, target) in enumerate(
            (
                (hub_hbm, hub_ref),
                (z_hbm, z_ref),
                (var_hbm, var_ref),
                (x_hbm, x_ref),
                (ties_hbm, ties_ref),
                (holder_hbm, holder_ref),
                (pos_hbm, pos_ref),
            )
        )
    ]
    for load in loads:
        load.start()

    barrier = pltpu.get_barrier_semaphore()

    def greet_area(i, carry):
        pl.semaphore_signal(
            barrier, inc=1, device_id=(lax.rem(a + i, areas), s), device_id_type=MESH
        )
        return carry

    def greet_snap(i, carry):
        pl.semaphore_signal(
            barrier, inc=1, device_id=(a, lax.rem(s + i, peers)), device_id_type=MESH
        )
        return carry

    lax.fori_loop(1, areas, greet_area, 0)
    lax.fori_loop(1, peers, greet_snap, 0)

    tiles_copy.start()
    gain_copy.start()

    for load in loads:
        load.wait()
    lane_a = lax.broadcasted_iota(i32, (areas, LANES), 1)
    for index, listing in enumerate((hub_ref, holder_ref)):
        both = jnp.concatenate([listing[...], listing[...]], axis=1)
        table[index] = both
    for block in range(nb):
        aug[block] = x_ref[:, block * LANES : (block + 1) * LANES].astype(bf16)
    aug[slots] = jnp.zeros((snaps, LANES), bf16)
    for step in range(ITERS):
        for side in range(2):
            br[step, side, ties] = jnp.zeros((snaps, LANES), f32)

    @pl.when(jnp.logical_not(has_lower))
    def _():
        for t in range(ties):
            aug[nb + t] = jnp.zeros((snaps, LANES), bf16)
            for step in range(ITERS):
                br[step, 0, t] = jnp.zeros((snaps, LANES), f32)

    @pl.when(jnp.logical_not(has_upper))
    def _():
        for t in range(ties):
            aug[nb + ties + t] = jnp.zeros((snaps, LANES), bf16)
            for step in range(ITERS):
                br[step, 1, t] = jnp.zeros((snaps, LANES), f32)

    pl.semaphore_wait(barrier, areas - 1 + peers - 1)

    def frontier_copy(step, side):
        return pltpu.make_async_remote_copy(
            src_ref=fs.at[step, side],
            dst_ref=fr.at[step, 1 - side],
            send_sem=f_send.at[step, side],
            recv_sem=f_recv.at[step, side],
            device_id=(a - 1 if side == 0 else a + 1, s),
            device_id_type=MESH,
        )

    def frontier_start(step):
        for side in range(2):
            for t in range(ties):
                entry = ties_ref[side, t]
                fs[step, side, t] = aug[jnp.where(entry >= 0, entry, slots)]

        @pl.when(has_lower)
        def _():
            frontier_copy(step, 0).start()

        @pl.when(has_upper)
        def _():
            frontier_copy(step, 1).start()

    def frontier_wait(step):
        @pl.when(has_lower)
        def _():
            frontier_copy(step, 1).wait_recv()
            for t in range(ties):
                aug[nb + t] = fr[step, 0, t]

        @pl.when(has_upper)
        def _():
            frontier_copy(step, 0).wait_recv()
            for t in range(ties):
                aug[nb + ties + t] = fr[step, 1, t]

    frontier_start(0)

    def rows_copy(i, source):
        first = pl.multiple_of(lax.rem(s + i, peers) * rows, rows)
        return pltpu.make_async_remote_copy(
            src_ref=x_ref.at[:, pl.ds(first, rows)],
            dst_ref=held.at[0, source],
            send_sem=x_send.at[i],
            recv_sem=x_recv.at[source],
            device_id=(a, lax.rem(s + i, peers)),
            device_id_type=MESH,
        )

    for i in range(1, peers):
        rows_copy(i, s).start()
    held[0, s] = x_ref[:, pl.ds(pl.multiple_of(s * rows, rows), rows)]

    def table_row(index, q):
        even = table[index, pl.ds(2 * q, 1), :]
        odd = table[index, pl.ds(2 * q + 1, 1), :]
        lane = lax.broadcasted_iota(i32, (1, LANES), 1)
        return jnp.where(lane < cap, even, odd)

    lane_h = lax.broadcasted_iota(i32, (half, LANES), 1)

    wide = min(chunks, 4)
    tall = chunks // wide

    def route_out(i, carry):
        k = lax.rem(i, tall)
        turn = (k + 1) // 2
        dy = tall // 2 + turn * (1 - 2 * (k % 2))
        group = lax.div(i, tall)
        dx = lax.rem(wide // 2 + group, wide)
        chip = lax.div(a, 2)
        q = lax.rem(lax.div(chip, wide) + dy, tall) * wide + lax.rem(lax.rem(chip, wide) + dx, wide)
        where_at = table_row(0, q)
        block_of = lax.shift_right_arithmetic(where_at, 7)
        lane_of = where_at & (LANES - 1)
        lanes = jnp.broadcast_to(lane_of, (snaps, LANES))
        from_block = jnp.broadcast_to(block_of, (snaps, LANES))
        taken = jnp.zeros((snaps, LANES), f32)
        for block in range(mb):
            found = jnp.take_along_axis(
                z_ref[:, block * LANES : (block + 1) * LANES], lanes, axis=1
            )
            taken = jnp.where(from_block == block, found, taken)
        low, high = taken[:half], taken[half:]
        zs[2 * q] = jnp.where(lane_h < cap, low, pltpu.roll(high, cap, 1))
        zs[2 * q + 1] = jnp.where(lane_h < cap, pltpu.roll(low, cap, 1), high)
        var_found = jnp.take_along_axis(
            var_ref[...], jnp.broadcast_to(lane_of, (mb, LANES)), axis=1
        )
        var_rows = lax.broadcasted_iota(i32, (mb, LANES), 0)
        vs[q] = jnp.sum(
            jnp.where(var_rows == jnp.broadcast_to(block_of, (mb, LANES)), var_found, 0.0),
            axis=0,
            keepdims=True,
        )
        for parity in range(2):
            d = 2 * q + parity

            @pl.when(d != a)
            def _():
                pltpu.make_async_remote_copy(
                    src_ref=zs.at[d],
                    dst_ref=zr.at[a],
                    send_sem=z_send,
                    recv_sem=z_recv.at[group],
                    device_id=(d, s),
                    device_id_type=MESH,
                ).start()
                pltpu.make_async_remote_copy(
                    src_ref=vs.at[q],
                    dst_ref=vr.at[a],
                    send_sem=v_send,
                    recv_sem=v_recv.at[group],
                    device_id=(d, s),
                    device_id_type=MESH,
                ).start()

            @pl.when(d == a)
            def _():
                pltpu.make_async_copy(zs.at[d], zr.at[a], z_recv.at[group]).start()
                pltpu.make_async_copy(vs.at[q], vr.at[a], v_recv.at[group]).start()

        return carry

    lax.fori_loop(0, chunks, route_out, 0, unroll=UNROLL[2])

    sub_q = lax.broadcasted_iota(i32, (mb, LANES), 0)
    lane_q = lax.broadcasted_iota(i32, (mb, LANES), 1)
    sub_l = lax.broadcasted_iota(i32, (LANES, LANES), 0)

    def invert(q, total):
        where_at = table_row(1, q)
        mine = jnp.broadcast_to(lax.shift_right_arithmetic(where_at, 7), (mb, LANES)) == sub_q
        left = jnp.concatenate(
            [jnp.where(mine, lane_q, 0).astype(f32), jnp.where(mine, q, 0).astype(f32)], axis=0
        ).astype(bf16)
        hit = jnp.broadcast_to(where_at & (LANES - 1), (LANES, LANES)) == sub_l
        right = jnp.where(hit, 1.0, 0.0).astype(bf16)
        return total + lax.dot_general(left, right, NT, preferred_element_type=f32)

    inverse = lax.fori_loop(
        0, chunks, invert, jnp.zeros((2 * mb, LANES), f32), unroll=UNROLL[0]
    )
    inv_lane[...] = inverse[:mb].astype(i32) & (LANES - 1)
    inv_q[...] = inverse[mb:].astype(i32)

    def index_tiles(n, carry):
        for j in range(mb):
            which = all_tiles
            for k in range(touched):
                tile = j * touched + k
                which = jnp.where(pos_ref[k, j] == n, tile, which)
            tile_index[n, j] = which
        return carry

    tiles_copy.wait()

    def predict(step):
        frontier_wait(step)

        def body(j, carry):
            total = jnp.zeros((snaps, LANES), f32)
            for k in range(touched):
                total += lax.dot_general(
                    aug[pos_ref[k, j]],
                    tiles[j * touched + k],
                    NT,
                    preferred_element_type=f32,
                )
            resid[j] = total
            return carry

        lax.fori_loop(0, mb, body, 0, unroll=min(mb, UNROLL[1]))

    predict(0)
    lax.fori_loop(0, slots, index_tiles, 0)
    part_grad[all_tiles] = jnp.zeros((snaps, LANES), f32)
    gain_copy.wait()
    gain_t[...] = gain[...].T

    my_wide = lax.rem(lax.div(a, 2), wide)
    batch = zr.at[pl.ds(0, 2 * tall)]
    batch_v = vr.at[pl.ds(0, 2 * tall)]
    sub_v = lax.broadcasted_iota(i32, (2 * tall, LANES), 0)
    my_half = lax.rem(a, 2) * cap
    for group in range(wide):
        from_wide = lax.rem(my_wide + 2 * wide - (wide // 2 + group) % wide, wide)
        pltpu.make_async_copy(batch, batch, z_recv.at[group]).wait()
        pltpu.make_async_copy(batch_v, batch_v, v_recv.at[group]).wait()
        variances = jnp.concatenate(
            [
                vr[2 * (row * wide + from_wide) + parity]
                for row in range(tall)
                for parity in range(2)
            ],
            axis=0,
        )

        def unpack(row, carry):
            q = row * wide + from_wide
            even, odd = zr[2 * q], zr[2 * q + 1]
            arrived[row, pl.ds(0, half)] = jnp.where(
                lane_h < cap, even, pltpu.roll(odd, cap, 1)
            )
            arrived[row, pl.ds(half, half)] = jnp.where(
                lane_h < cap, pltpu.roll(even, cap, 1), odd
            )
            return carry

        lax.fori_loop(0, tall, unpack, 0, unroll=True)

        def reorder(j, carry):
            lanes = jnp.broadcast_to(inv_lane[pl.ds(j, 1), :], (snaps, LANES))
            from_chunk = jnp.broadcast_to(inv_q[pl.ds(j, 1), :], (snaps, LANES))
            taken = jnp.zeros((snaps, LANES), f32) if group == 0 else z_own[j]
            for row in range(tall):
                found = jnp.take_along_axis(arrived[row], lanes, axis=1)
                taken = jnp.where(from_chunk == row * wide + from_wide, found, taken)
            z_own[j] = taken
            lane_of = inv_lane[pl.ds(j, 1), :]
            chunk_of = inv_q[pl.ds(j, 1), :]
            place = 2 * lax.shift_right_arithmetic(chunk_of, wide.bit_length() - 1)
            place += lax.shift_right_arithmetic(lane_of, 6)
            place = jnp.where((chunk_of & (wide - 1)) == from_wide, place, -1)
            found = jnp.take_along_axis(
                variances,
                jnp.broadcast_to((lane_of & (cap - 1)) + my_half, (2 * tall, LANES)),
                axis=1,
            )
            part = jnp.sum(
                jnp.where(jnp.broadcast_to(place, (2 * tall, LANES)) == sub_v, found, 0.0),
                axis=0,
                keepdims=True,
            )
            v_own[pl.ds(j, 1), :] = part if group == 0 else v_own[pl.ds(j, 1), :] + part
            return carry

        lax.fori_loop(0, mb, reorder, 0, unroll=min(mb, 4))

    def spread_copy(step, i):
        peer = lax.rem(s + i, peers)
        return pltpu.make_async_remote_copy(
            src_ref=ssr.at[step, s],
            dst_ref=ssr.at[step, s],
            send_sem=s_send.at[step, i],
            recv_sem=s_recv.at[step, s],
            device_id=(a, peer),
            device_id_type=MESH,
        )

    def spread_wait(step, i):
        source = lax.rem(s + i, peers)
        pltpu.make_async_remote_copy(
            src_ref=ssr.at[step, source],
            dst_ref=ssr.at[step, source],
            send_sem=s_send.at[step, i],
            recv_sem=s_recv.at[step, source],
            device_id=(a, source),
            device_id_type=MESH,
        ).wait_recv()

    def boundary_copy(step, side, part):
        return pltpu.make_async_remote_copy(
            src_ref=bs.at[step, side, pl.ds(2 * part, 2)],
            dst_ref=br.at[step, 1 - side, pl.ds(2 * part, 2)],
            send_sem=b_send.at[step, side, part],
            recv_sem=b_recv.at[step, side, part],
            device_id=(a - 1 if side == 0 else a + 1, s),
            device_id_type=MESH,
        )

    def ring_copy(step, way, hop, piece, chunk):
        beside = lax.rem(s + 1, peers) if way == 0 else lax.rem(s + peers - 1, peers)
        part = pl.ds(piece * piece_units, piece_units)
        return pltpu.make_async_remote_copy(
            src_ref=gath.at[step, chunk, part],
            dst_ref=gath.at[step, chunk, part],
            send_sem=ring_send.at[step, way, hop - 1, piece],
            recv_sem=ring_recv.at[step, way, hop - 1, piece],
            device_id=(a, beside),
            device_id_type=MESH,
        )

    def ring_pieces(way, hop):
        if hop < reach:
            return range(pieces)
        return range(pieces // 2) if way == 0 else range(pieces // 2, pieces)

    def piece_of(way, turn):
        return turn if way == 0 else (turn + pieces // 2) % pieces

    arrivals = [(hop, turn) for hop in range(1, reach) for turn in range(pieces)]
    arrivals += [(reach, turn) for turn in range(pieces // 2)]
    if (reach, pieces) == (4, 4):
        arrivals = ARRIVALS

    def came_from(way, hop):
        return lax.rem(s + peers - hop, peers) if way == 0 else lax.rem(s + hop, peers)

    def update_copy(step, chunk):
        return pltpu.make_async_remote_copy(
            src_ref=us.at[step, chunk],
            dst_ref=ur.at[step, s],
            send_sem=u_send.at[step, chunk],
            recv_sem=u_recv.at[step, s],
            device_id=(a, chunk),
            device_id_type=MESH,
        )

    def tile_products():
        def body(j, carry):
            for k in range(0, touched, 2):
                pair = jnp.dot(
                    wgt[j],
                    jnp.concatenate(
                        [tiles[j * touched + k], tiles[j * touched + k + 1]], axis=1
                    ),
                    preferred_element_type=f32,
                )
                part_grad[j * touched + k] = pair[:, :LANES]
                part_grad[j * touched + k + 1] = pair[:, LANES:]
            return carry

        lax.fori_loop(0, mb, body, 0, unroll=min(mb, 8))

    def slot_sum(n):
        terms = [part_grad[tile_index[n, j]] for j in range(mb)]
        while len(terms) > 1:
            terms = [
                terms[i] + terms[i + 1] if i + 1 < len(terms) else terms[i]
                for i in range(0, len(terms), 2)
            ]
        return terms[0]

    def gain_piece(step, chunk, piece):
        total = jnp.zeros((snaps, rows), f32)
        for u in range(piece * piece_units, (piece + 1) * piece_units):
            total += jnp.dot(
                gath[step, chunk, u],
                gain_t[u * 2 * LANES : (u + 1) * 2 * LANES, :],
                preferred_element_type=f32,
            )
        return total

    def returned(step, chunk, update):
        if step + 1 < ITERS:
            held[1, chunk] = update
            return (held[0, chunk] + update).astype(bf16)
        return (held[1, chunk] + update).astype(bf16)

    for step in range(ITERS):
        if step > 0:
            frontier_start(step)
            predict(step)

        for j in range(mb):
            left_over = z_own[j] - resid[j]
            resid[j] = left_over
            ssr[step, s, pl.ds(j, 1), :] = jnp.sum(
                left_over * left_over, axis=0, keepdims=True
            )
        for i in range(1, peers):
            spread_copy(step, i).start()
        for i in range(1, peers):
            spread_wait(step, i)
        total = ssr[step, 0]
        for i in range(1, peers):
            total += ssr[step, i]
        scale = v_own[...] + total / snaps_all
        for j in range(mb):
            wgt[j] = (resid[j] / scale[j : j + 1, :]).astype(bf16)

        tile_products()
        for side in range(2):
            for part in range(ties // 2):
                for t in (2 * part, 2 * part + 1):
                    bs[step, side, t] = slot_sum(nb + side * ties + t)

                @pl.when(has_lower if side == 0 else has_upper)
                def _():
                    boundary_copy(step, side, part).start()

        def own_slots(n, carry):
            grads[n] = slot_sum(n)
            return carry

        lax.fori_loop(0, nb, own_slots, 0, unroll=4)

        @pl.when(has_upper)
        def _():
            for part in range(ties // 2):
                boundary_copy(step, 0, part).wait_recv()

        @pl.when(has_lower)
        def _():
            for part in range(ties // 2):
                boundary_copy(step, 1, part).wait_recv()

        for turn in range(pieces // 2):
            for way in range(2):
                piece = piece_of(way, turn)
                for block in range(2 * piece_units * piece, 2 * piece_units * (piece + 1)):
                    total = grads[block]
                    for side in range(2):
                        which = ties
                        for t in range(ties):
                            which = jnp.where(ties_ref[side, t] == block, t, which)
                        total += br[step, side, which]
                    first = (block % 2) * LANES
                    gath[step, s, block // 2, :, first : first + LANES] = total.astype(bf16)
                ring_copy(step, way, 1, piece, s).start()
        for turn in range(pieces // 2, pieces):
            for way in range(2):
                ring_copy(step, way, 1, piece_of(way, turn), s).start()

        own = gain_piece(step, s, 0)
        for piece in range(1, pieces):
            own += gain_piece(step, s, piece)
        if step == 0:
            for i in range(1, peers):
                rows_copy(i, lax.rem(s + i, peers)).wait_recv()
        ur[step, s] = returned(step, s, own)

        sums = {}
        for hop, turn in arrivals:
            for way in range(2):
                piece = piece_of(way, turn)
                chunk = came_from(way, hop)
                ring_copy(step, way, hop, piece, chunk).wait_recv()
                if hop < reach and piece in ring_pieces(way, hop + 1):
                    ring_copy(step, way, hop + 1, piece, chunk).start()
            for way in range(2):
                chunk = came_from(way, hop)
                part = gain_piece(step, chunk, piece_of(way, turn))
                key = (hop, way if hop < reach else 0)
                count, total = sums.get(key, (0, 0.0))
                sums[key] = count + 1, total + part
                if count + 1 == pieces:
                    us[step, chunk] = returned(step, chunk, total + part)
                    update_copy(step, chunk).start()

        for i in range(peers):

            @pl.when(i != s)
            def _():
                pltpu.make_async_remote_copy(
                    src_ref=us.at[step, i],
                    dst_ref=ur.at[step, i],
                    send_sem=u_send.at[step, i],
                    recv_sem=u_recv.at[step, i],
                    device_id=(a, i),
                    device_id_type=MESH,
                ).wait_recv()

        for i in range(peers):
            if step + 1 < ITERS:
                for r in range(rows // LANES):
                    aug[i * (rows // LANES) + r] = ur[
                        step, i, :, r * LANES : (r + 1) * LANES
                    ]
            else:
                cols = slice(i * rows, (i + 1) * rows)
                out_ref[:, cols] = x_ref[:, cols] + ur[step, i].astype(f32)

    for i in range(1, peers):
        rows_copy(i, s).wait_send()
    pltpu.make_async_copy(
        zs.at[pl.ds(0, areas - 1)], zr.at[pl.ds(0, areas - 1)], z_send
    ).wait()
    pltpu.make_async_copy(
        vr.at[pl.ds(0, areas - 1)], vr.at[pl.ds(0, areas - 1)], v_send
    ).wait()
    for step in range(ITERS):

        @pl.when(has_lower)
        def _():
            frontier_copy(step, 0).wait_send()
            for part in range(ties // 2):
                boundary_copy(step, 0, part).wait_send()

        @pl.when(has_upper)
        def _():
            frontier_copy(step, 1).wait_send()
            for part in range(ties // 2):
                boundary_copy(step, 1, part).wait_send()

        for i in range(1, peers):
            spread_copy(step, i).wait_send()
            update_copy(step, lax.rem(s + i, peers)).wait_send()
        for way in range(2):
            for hop in range(1, reach + 1):
                for piece in ring_pieces(way, hop):
                    ring_copy(step, way, hop, piece, s).wait_send()


def on_device(
    phasor_readings,
    reading_error_spread,
    starting_voltages,
    derivative_pieces,
    derivative_tile_position,
    frontier_voltage_pieces,
    holder_line_order,
    hub_line_order,
    reciprocal_normal_operator,
):
    areas, peers = lax.axis_size("area"), lax.axis_size("snap")
    snaps, states = starting_voltages.shape
    nb = states // LANES
    mb, touched = derivative_tile_position.shape[1:]
    ties = frontier_voltage_pieces.shape[2]
    cap = holder_line_order.shape[2]
    rows = states // peers
    chunks = areas * cap // LANES
    slots = nb + 2 * ties
    all_tiles = mb * touched
    units = nb // 2
    reach = peers // 2
    pieces = units // 2
    f32, bf16, i32 = jnp.float32, jnp.bfloat16, jnp.int32
    vmem = pl.BlockSpec(memory_space=pltpu.VMEM)
    hbm = pl.BlockSpec(memory_space=pltpu.HBM)
    dma = pltpu.SemaphoreType.DMA
    dims = (areas, peers, snaps, nb, mb, touched, ties, cap)
    return pl.pallas_call(
        functools.partial(step_kernel, dims),
        out_shape=jax.ShapeDtypeStruct((snaps, states), f32),
        in_specs=[hbm] * 9,
        out_specs=vmem,
        scratch_shapes=[
            pltpu.VMEM((snaps, mb * LANES), f32),
            pltpu.VMEM((mb, LANES), f32),
            pltpu.VMEM((snaps, states), f32),
            pltpu.SMEM((touched, mb), i32),
            pltpu.SMEM((2, ties), i32),
            pltpu.VMEM((areas, cap), i32),
            pltpu.VMEM((areas, cap), i32),
            dma((7,)),
            pltpu.VMEM((all_tiles, LANES, LANES), bf16),
            pltpu.VMEM((rows, states), bf16),
            pltpu.VMEM((states, rows), bf16),
            pltpu.SMEM((slots, mb), i32),
            pltpu.VMEM((2, areas, LANES), i32),
            pltpu.VMEM((areas, snaps // 2, LANES), f32),
            pltpu.VMEM((areas, snaps // 2, LANES), f32),
            pltpu.VMEM((chunks, 1, LANES), f32),
            pltpu.VMEM((areas, 1, LANES), f32),
            pltpu.VMEM((chunks // min(chunks, 4), snaps, LANES), f32),
            pltpu.VMEM((mb, LANES), i32),
            pltpu.VMEM((mb, LANES), i32),
            pltpu.VMEM((mb, snaps, LANES), f32),
            pltpu.VMEM((mb, LANES), f32),
            pltpu.VMEM((slots + 1, snaps, LANES), bf16),
            pltpu.VMEM((ITERS, 2, ties, snaps, LANES), bf16),
            pltpu.VMEM((ITERS, 2, ties, snaps, LANES), bf16),
            pltpu.VMEM((mb, snaps, LANES), f32),
            pltpu.VMEM((ITERS, peers, mb, LANES), f32),
            pltpu.VMEM((mb, snaps, LANES), bf16),
            pltpu.VMEM((nb, snaps, LANES), f32),
            pltpu.VMEM((ITERS, 2, ties, snaps, LANES), f32),
            pltpu.VMEM((ITERS, 2, ties + 1, snaps, LANES), f32),
            pltpu.VMEM((ITERS, peers, units, snaps, 2 * LANES), bf16),
            pltpu.VMEM((ITERS, peers, snaps, rows), bf16),
            pltpu.VMEM((ITERS, peers, snaps, rows), bf16),
            pltpu.VMEM((2, peers, snaps, rows), f32),
            pltpu.VMEM((all_tiles + 1, snaps, LANES), f32),
            dma((2,)),
            dma((peers,)),
            dma((peers,)),
            dma(()),
            dma((min(chunks, 4),)),
            dma(()),
            dma((min(chunks, 4),)),
            dma((ITERS, 2)),
            dma((ITERS, 2)),
            dma((ITERS, peers)),
            dma((ITERS, peers)),
            dma((ITERS, 2, ties // 2)),
            dma((ITERS, 2, ties // 2)),
            dma((ITERS, 2, reach, pieces)),
            dma((ITERS, 2, reach, pieces)),
            dma((ITERS, peers)),
            dma((ITERS, peers)),
        ],
        compiler_params=pltpu.CompilerParams(collective_id=0, has_side_effects=True),
        name="estimate",
    )(
        phasor_readings,
        reading_error_spread.reshape(mb, LANES),
        starting_voltages,
        derivative_pieces.reshape(all_tiles, LANES, LANES),
        derivative_tile_position[0].T,
        frontier_voltage_pieces[0],
        holder_line_order[0],
        hub_line_order[0],
        reciprocal_normal_operator,
    )


def solution(mesh):
    placed = (
        P("snap", "area"),
        P("area"),
        P("snap", "area"),
        P("area", None, None, None),
        P("area", None, None),
        P("area", None, None),
        P("area", None, None),
        P("area", None, None),
        P(("area", "snap"), None),
    )
    return jax.shard_map(
        on_device, mesh=mesh, in_specs=placed, out_specs=P("snap", "area"), check_vma=False
    )
```

```python
import functools

import jax
import jax.numpy as jnp
from jax import lax
from jax.experimental import pallas as pl
from jax.experimental.pallas import tpu as pltpu
from jax.sharding import PartitionSpec as P

ITERS = 2
UNROLL = (8, 8, 4)
GAIN_PARTS = 4
GAIN_EARLY = 3
LANES = 128
MESH = pl.DeviceIdType.MESH
NT = (((1,), (1,)), ((), ()))


def step_kernel(
    dims,
    z_hbm,
    var_hbm,
    x_hbm,
    tiles_hbm,
    pos_hbm,
    ties_hbm,
    holder_hbm,
    hub_hbm,
    gain_hbm,
    out_ref,
    z_ref,
    var_ref,
    x_ref,
    pos_ref,
    ties_ref,
    holder_ref,
    hub_ref,
    load_sem,
    tiles,
    gain,
    tile_index,
    table,
    zs,
    zr,
    arrived,
    inv_q,
    inv_lane,
    z_own,
    v_own,
    aug,
    fs,
    fr,
    resid,
    ssr,
    wgt,
    grads,
    bs,
    br,
    gath,
    us,
    ur,
    held,
    part_grad,
    g_send,
    g_recv,
    local_sem,
    x_send,
    x_recv,
    z_send,
    z_recv,
    f_send,
    f_recv,
    s_send,
    s_recv,
    b_send,
    b_recv,
    ring_send,
    ring_recv,
    u_send,
    u_recv,
):
    areas, peers, snaps, nb, mb, touched, ties, cap = dims
    half = snaps // 2
    chunks = areas * cap // LANES
    rows = nb * LANES // peers
    units = nb // 2
    piece_units = 2
    pieces = units // piece_units
    slots = nb + 2 * ties
    all_tiles = mb * touched
    snaps_all = snaps * peers
    f32, bf16, i32 = jnp.float32, jnp.bfloat16, jnp.int32

    a = lax.axis_index("area")
    s = lax.axis_index("snap")
    has_lower = a > 0
    has_upper = a < areas - 1

    tiles_copy = pltpu.make_async_copy(
        tiles_hbm, tiles, local_sem.at[0]
    )
    gain_copy = pltpu.make_async_copy(gain_hbm, gain.at[0], local_sem.at[1])
    loads = [
        pltpu.make_async_copy(source, target, load_sem.at[i])
        for i, (source, target) in enumerate(
            (
                (hub_hbm, hub_ref),
                (z_hbm, z_ref),
                (var_hbm, var_ref),
                (x_hbm, x_ref),
                (ties_hbm, ties_ref),
                (holder_hbm, holder_ref),
                (pos_hbm, pos_ref),
            )
        )
    ]
    for load in loads:
        load.start()

    barrier = pltpu.get_barrier_semaphore()

    def greet_area(i, carry):
        pl.semaphore_signal(
            barrier, inc=1, device_id=(lax.rem(a + i, areas), s), device_id_type=MESH
        )
        return carry

    def greet_snap(i, carry):
        pl.semaphore_signal(
            barrier, inc=1, device_id=(a, lax.rem(s + i, peers)), device_id_type=MESH
        )
        return carry

    lax.fori_loop(1, areas, greet_area, 0)
    lax.fori_loop(1, peers, greet_snap, 0)

    tiles_copy.start()
    gain_copy.start()

    for load in loads:
        load.wait()
    lane_a = lax.broadcasted_iota(i32, (areas, LANES), 1)
    for index, listing in enumerate((hub_ref, holder_ref)):
        both = jnp.concatenate([listing[...], listing[...]], axis=1)
        table[index] = both
    for block in range(nb):
        aug[block] = x_ref[:, block * LANES : (block + 1) * LANES].astype(bf16)
    aug[slots] = jnp.zeros((snaps, LANES), bf16)
    for step in range(ITERS):
        for side in range(2):
            br[step, side, ties] = jnp.zeros((snaps, LANES), f32)

    @pl.when(jnp.logical_not(has_lower))
    def _():
        for t in range(ties):
            aug[nb + t] = jnp.zeros((snaps, LANES), bf16)
            for step in range(ITERS):
                br[step, 0, t] = jnp.zeros((snaps, LANES), f32)

    @pl.when(jnp.logical_not(has_upper))
    def _():
        for t in range(ties):
            aug[nb + ties + t] = jnp.zeros((snaps, LANES), bf16)
            for step in range(ITERS):
                br[step, 1, t] = jnp.zeros((snaps, LANES), f32)

    pl.semaphore_wait(barrier, areas - 1 + peers - 1)

    def frontier_copy(step, side):
        return pltpu.make_async_remote_copy(
            src_ref=fs.at[step, side],
            dst_ref=fr.at[step, 1 - side],
            send_sem=f_send.at[step, side],
            recv_sem=f_recv.at[step, side],
            device_id=(a - 1 if side == 0 else a + 1, s),
            device_id_type=MESH,
        )

    def frontier_start(step):
        for side in range(2):
            for t in range(ties):
                entry = ties_ref[side, t]
                fs[step, side, t] = aug[jnp.where(entry >= 0, entry, slots)]

        @pl.when(has_lower)
        def _():
            frontier_copy(step, 0).start()

        @pl.when(has_upper)
        def _():
            frontier_copy(step, 1).start()

    def frontier_wait(step):
        @pl.when(has_lower)
        def _():
            frontier_copy(step, 1).wait_recv()
            for t in range(ties):
                aug[nb + t] = fr[step, 0, t]

        @pl.when(has_upper)
        def _():
            frontier_copy(step, 0).wait_recv()
            for t in range(ties):
                aug[nb + ties + t] = fr[step, 1, t]

    frontier_start(0)

    ahead = 1 - 2 * lax.rem(a, 2)

    def along(distance):
        return lax.rem(s + distance * ahead + 2 * peers, peers)

    def block_of_rows(device, index):
        shift = (0, -1, 1)[index]
        return lax.rem(device + shift * ahead + peers, peers)

    target = {1: along(3), 2: along(-2)}
    source = {1: along(-3), 2: along(2)}
    held_blocks = {0: 3, 1: 3, 2: 2}
    part_height = rows // GAIN_PARTS

    def gain_copy_to(side, part):
        where = pl.ds(part * part_height, part_height)
        return pltpu.make_async_remote_copy(
            src_ref=gain_hbm.at[where],
            dst_ref=gain.at[1 + side, where],
            send_sem=g_send.at[side, part],
            recv_sem=g_recv.at[side, part],
            device_id=(a, along(1) if side == 0 else along(-1)),
            device_id_type=MESH,
        )

    def columns_of(block):
        return pl.ds(pl.multiple_of(block * rows, rows), rows)

    def rows_copy(role, index):
        block = block_of_rows(target[role], index)
        return pltpu.make_async_remote_copy(
            src_ref=x_ref.at[:, columns_of(block)],
            dst_ref=held.at[0, role, index],
            send_sem=x_send.at[role, index],
            recv_sem=x_recv.at[role, index],
            device_id=(a, target[role]),
            device_id_type=MESH,
        )

    for role in (1, 2):
        for index in range(held_blocks[role]):
            rows_copy(role, index).start()
    for part in range(GAIN_EARLY):
        for side in range(2):
            gain_copy_to(side, part).start()
    for index in range(3):
        held[0, 0, index] = x_ref[:, columns_of(block_of_rows(s, index))]

    def table_row(index, q):
        even = table[index, pl.ds(2 * q, 1), :]
        odd = table[index, pl.ds(2 * q + 1, 1), :]
        lane = lax.broadcasted_iota(i32, (1, LANES), 1)
        return jnp.where(lane < cap, even, odd)

    lane_h = lax.broadcasted_iota(i32, (half, LANES), 1)

    wide = min(chunks, 4)
    tall = chunks // wide

    def route_out(i, carry):
        k = lax.rem(i, tall)
        turn = (k + 1) // 2
        dy = tall // 2 + turn * (1 - 2 * (k % 2))
        group = lax.div(i, tall)
        dx = lax.rem(wide // 2 + group, wide)
        chip = lax.div(a, 2)
        q = lax.rem(lax.div(chip, wide) + dy, tall) * wide + lax.rem(lax.rem(chip, wide) + dx, wide)
        where_at = table_row(0, q)
        block_of = lax.shift_right_arithmetic(where_at, 7)
        lane_of = where_at & (LANES - 1)
        lanes = jnp.broadcast_to(lane_of, (snaps, LANES))
        from_block = jnp.broadcast_to(block_of, (snaps, LANES))
        taken = jnp.zeros((snaps, LANES), f32)
        for block in range(mb):
            found = jnp.take_along_axis(
                z_ref[:, block * LANES : (block + 1) * LANES], lanes, axis=1
            )
            taken = jnp.where(from_block == block, found, taken)
        low, high = taken[:half], taken[half:]
        zs[2 * q, pl.ds(0, half)] = jnp.where(lane_h < cap, low, pltpu.roll(high, cap, 1))
        zs[2 * q + 1, pl.ds(0, half)] = jnp.where(lane_h < cap, pltpu.roll(low, cap, 1), high)
        var_found = jnp.take_along_axis(
            var_ref[...], jnp.broadcast_to(lane_of, (mb, LANES)), axis=1
        )
        var_rows = lax.broadcasted_iota(i32, (mb, LANES), 0)
        var_row = jnp.sum(
            jnp.where(var_rows == jnp.broadcast_to(block_of, (mb, LANES)), var_found, 0.0),
            axis=0,
            keepdims=True,
        )
        for parity in range(2):
            d = 2 * q + parity
            zs[d, pl.ds(half, 1)] = var_row

            @pl.when(d != a)
            def _():
                pltpu.make_async_remote_copy(
                    src_ref=zs.at[d],
                    dst_ref=zr.at[a],
                    send_sem=z_send,
                    recv_sem=z_recv.at[group],
                    device_id=(d, s),
                    device_id_type=MESH,
                ).start()

            @pl.when(d == a)
            def _():
                pltpu.make_async_copy(zs.at[d], zr.at[a], z_recv.at[group]).start()

        return carry

    lax.fori_loop(0, chunks, route_out, 0, unroll=UNROLL[2])

    sub_q = lax.broadcasted_iota(i32, (mb, LANES), 0)
    lane_q = lax.broadcasted_iota(i32, (mb, LANES), 1)
    sub_l = lax.broadcasted_iota(i32, (LANES, LANES), 0)

    def invert(q, total):
        where_at = table_row(1, q)
        mine = jnp.broadcast_to(lax.shift_right_arithmetic(where_at, 7), (mb, LANES)) == sub_q
        left = jnp.concatenate(
            [jnp.where(mine, lane_q, 0).astype(f32), jnp.where(mine, q, 0).astype(f32)], axis=0
        ).astype(bf16)
        hit = jnp.broadcast_to(where_at & (LANES - 1), (LANES, LANES)) == sub_l
        right = jnp.where(hit, 1.0, 0.0).astype(bf16)
        return total + lax.dot_general(left, right, NT, preferred_element_type=f32)

    inverse = lax.fori_loop(
        0, chunks, invert, jnp.zeros((2 * mb, LANES), f32), unroll=UNROLL[0]
    )
    inv_lane[...] = inverse[:mb].astype(i32) & (LANES - 1)
    inv_q[...] = inverse[mb:].astype(i32)

    def index_tiles(n, carry):
        for j in range(mb):
            which = all_tiles
            for k in range(touched):
                tile = j * touched + k
                which = jnp.where(pos_ref[k, j] == n, tile, which)
            tile_index[n, j] = which
        return carry

    tiles_copy.wait()

    def predict(mine):
        def body(j, carry):
            total = jnp.zeros((snaps, LANES), f32)
            for k in range(touched):
                total += lax.dot_general(
                    aug[pos_ref[k, j]],
                    tiles[j * touched + k],
                    NT,
                    preferred_element_type=f32,
                )
            resid[j] = total
            return carry

        lax.fori_loop(mine.start, mine.stop, body, 0, unroll=min(len(mine), UNROLL[1]))

    frontier_wait(0)
    predict(range(mb))
    lax.fori_loop(0, slots, index_tiles, 0)
    part_grad[all_tiles] = jnp.zeros((snaps, LANES), f32)
    gain_copy.wait()

    my_wide = lax.rem(lax.div(a, 2), wide)
    batch = zr.at[pl.ds(0, 2 * tall)]
    sub_v = lax.broadcasted_iota(i32, (2 * tall, LANES), 0)
    my_half = lax.rem(a, 2) * cap
    for group in range(wide):
        from_wide = lax.rem(my_wide + 2 * wide - (wide // 2 + group) % wide, wide)
        pltpu.make_async_copy(batch, batch, z_recv.at[group]).wait()
        variances = jnp.concatenate(
            [
                zr[2 * (row * wide + from_wide) + parity, pl.ds(half, 1)]
                for row in range(tall)
                for parity in range(2)
            ],
            axis=0,
        )

        def unpack(row, carry):
            q = row * wide + from_wide
            even, odd = zr[2 * q, pl.ds(0, half)], zr[2 * q + 1, pl.ds(0, half)]
            arrived[row, pl.ds(0, half)] = jnp.where(
                lane_h < cap, even, pltpu.roll(odd, cap, 1)
            )
            arrived[row, pl.ds(half, half)] = jnp.where(
                lane_h < cap, pltpu.roll(even, cap, 1), odd
            )
            return carry

        lax.fori_loop(0, tall, unpack, 0, unroll=True)

        def reorder(j, carry):
            lanes = jnp.broadcast_to(inv_lane[pl.ds(j, 1), :], (snaps, LANES))
            from_chunk = jnp.broadcast_to(inv_q[pl.ds(j, 1), :], (snaps, LANES))
            taken = jnp.zeros((snaps, LANES), f32) if group == 0 else z_own[j]
            for row in range(tall):
                found = jnp.take_along_axis(arrived[row], lanes, axis=1)
                taken = jnp.where(from_chunk == row * wide + from_wide, found, taken)
            z_own[j] = taken
            lane_of = inv_lane[pl.ds(j, 1), :]
            chunk_of = inv_q[pl.ds(j, 1), :]
            place = 2 * lax.shift_right_arithmetic(chunk_of, wide.bit_length() - 1)
            place += lax.shift_right_arithmetic(lane_of, 6)
            place = jnp.where((chunk_of & (wide - 1)) == from_wide, place, -1)
            found = jnp.take_along_axis(
                variances,
                jnp.broadcast_to((lane_of & (cap - 1)) + my_half, (2 * tall, LANES)),
                axis=1,
            )
            part = jnp.sum(
                jnp.where(jnp.broadcast_to(place, (2 * tall, LANES)) == sub_v, found, 0.0),
                axis=0,
                keepdims=True,
            )
            v_own[pl.ds(j, 1), :] = part if group == 0 else v_own[pl.ds(j, 1), :] + part
            return carry

        lax.fori_loop(0, mb, reorder, 0, unroll=min(mb, 4))

    spread_parts = 2 if mb % 16 == 0 else 1
    part_rows = mb // spread_parts

    def spread_copy(step, i, part):
        where = pl.ds(part * part_rows, part_rows)
        peer = lax.rem(s + i, peers)
        return pltpu.make_async_remote_copy(
            src_ref=ssr.at[step, s, where],
            dst_ref=ssr.at[step, s, where],
            send_sem=s_send.at[step, i, part],
            recv_sem=s_recv.at[step, s, part],
            device_id=(a, peer),
            device_id_type=MESH,
        )

    def spread_wait(step, i, part):
        source = lax.rem(s + i, peers)
        where = pl.ds(part * part_rows, part_rows)
        pltpu.make_async_remote_copy(
            src_ref=ssr.at[step, source, where],
            dst_ref=ssr.at[step, source, where],
            send_sem=s_send.at[step, i, part],
            recv_sem=s_recv.at[step, source, part],
            device_id=(a, source),
            device_id_type=MESH,
        ).wait_recv()

    def boundary_copy(step, side, part):
        return pltpu.make_async_remote_copy(
            src_ref=bs.at[step, side, pl.ds(2 * part, 2)],
            dst_ref=br.at[step, 1 - side, pl.ds(2 * part, 2)],
            send_sem=b_send.at[step, side, part],
            recv_sem=b_recv.at[step, side, part],
            device_id=(a - 1 if side == 0 else a + 1, s),
            device_id_type=MESH,
        )

    def chunk_copy(step, role, piece):
        part = pl.ds(piece * piece_units, piece_units)
        return pltpu.make_async_remote_copy(
            src_ref=gath.at[step, 0, part],
            dst_ref=gath.at[step, role, part],
            send_sem=ring_send.at[step, role, piece],
            recv_sem=ring_recv.at[step, role, piece],
            device_id=(a, target[role]),
            device_id_type=MESH,
        )

    def update_copy(step, role, index):
        return pltpu.make_async_remote_copy(
            src_ref=us.at[step, role, index],
            dst_ref=ur.at[step, block_of_rows(s, index)],
            send_sem=u_send.at[step, role, index],
            recv_sem=u_recv.at[step, role, index],
            device_id=(a, source[role]),
            device_id_type=MESH,
        )

    def tile_products(mine):
        def body(j, carry):
            for k in range(0, touched, 2):
                pair = jnp.dot(
                    wgt[j],
                    jnp.concatenate(
                        [tiles[j * touched + k], tiles[j * touched + k + 1]], axis=1
                    ),
                    preferred_element_type=f32,
                )
                part_grad[j * touched + k] = pair[:, :LANES]
                part_grad[j * touched + k + 1] = pair[:, LANES:]
            return carry

        lax.fori_loop(mine.start, mine.stop, body, 0, unroll=min(len(mine), 8))

    def slot_sum(n):
        terms = [part_grad[tile_index[n, j]] for j in range(mb)]
        while len(terms) > 1:
            terms = [
                terms[i] + terms[i + 1] if i + 1 < len(terms) else terms[i]
                for i in range(0, len(terms), 2)
            ]
        return terms[0]

    def gain_piece(step, role, piece, sums):
        for index in range(held_blocks[role]):
            for u in range(piece * piece_units, (piece + 1) * piece_units):
                part = lax.dot_general(
                    gath[step, role, u],
                    gain[index, :, u * 2 * LANES : (u + 1) * 2 * LANES],
                    NT,
                    preferred_element_type=f32,
                )
                sums[role, index] = sums[role, index] + part if (role, index) in sums else part

    def returned(step, role, index, update):
        if step + 1 < ITERS:
            held[1, role, index] = update
            return (held[0, role, index] + update).astype(bf16)
        return (held[1, role, index] + update).astype(bf16)

    for step in range(ITERS):
        if step > 0:
            frontier_start(step)
            frontier_wait(step)
        for part in range(spread_parts):
            mine = range(part * part_rows, (part + 1) * part_rows)
            if step > 0:
                predict(mine)
            for j in mine:
                left_over = z_own[j] - resid[j]
                resid[j] = left_over
                ssr[step, s, pl.ds(j, 1), :] = jnp.sum(
                    left_over * left_over, axis=0, keepdims=True
                )
            for i in range(1, peers):
                spread_copy(step, i, part).start()
        if step == 0:
            for part in range(GAIN_EARLY, GAIN_PARTS):
                for side in range(2):
                    gain_copy_to(side, part).start()
        for part in range(spread_parts):
            mine = range(part * part_rows, (part + 1) * part_rows)
            for i in range(1, peers):
                spread_wait(step, i, part)
            where = pl.ds(part * part_rows, part_rows)
            total = ssr[step, 0, where]
            for i in range(1, peers):
                total += ssr[step, i, where]
            scale = v_own[where, :] + total / snaps_all
            for j in mine:
                row = j - part * part_rows
                wgt[j] = (resid[j] / scale[row : row + 1, :]).astype(bf16)
            tile_products(mine)
        for side in range(2):
            for part in range(ties // 2):
                for t in (2 * part, 2 * part + 1):
                    bs[step, side, t] = slot_sum(nb + side * ties + t)

                @pl.when(has_lower if side == 0 else has_upper)
                def _():
                    boundary_copy(step, side, part).start()

        def own_slots(n, carry):
            grads[n] = slot_sum(n)
            return carry

        lax.fori_loop(0, nb, own_slots, 0, unroll=4)

        @pl.when(has_upper)
        def _():
            for part in range(ties // 2):
                boundary_copy(step, 0, part).wait_recv()

        @pl.when(has_lower)
        def _():
            for part in range(ties // 2):
                boundary_copy(step, 1, part).wait_recv()

        for piece in range(pieces):
            for block in range(2 * piece_units * piece, 2 * piece_units * (piece + 1)):
                total = grads[block]
                for side in range(2):
                    which = ties
                    for t in range(ties):
                        which = jnp.where(ties_ref[side, t] == block, t, which)
                    total += br[step, side, which]
                first = (block % 2) * LANES
                gath[step, 0, block // 2, :, first : first + LANES] = total.astype(bf16)
            for role in (1, 2):
                chunk_copy(step, role, piece).start()

        if step == 0:
            for side in range(2):
                for part in range(GAIN_PARTS):
                    gain_copy_to(side, part).wait_recv()
            for role in (1, 2):
                for index in range(held_blocks[role]):
                    rows_copy(role, index).wait_recv()
        sums = {}
        for piece in range(pieces):
            gain_piece(step, 0, piece, sums)
        for index in range(3):
            ur[step, block_of_rows(s, index)] = returned(step, 0, index, sums[0, index])
        for piece in range(pieces):
            for role in (2, 1):
                chunk_copy(step, role, piece).wait_recv()
                gain_piece(step, role, piece, sums)
                if piece + 1 == pieces:
                    for index in range(held_blocks[role]):
                        us[step, role, index] = returned(step, role, index, sums[role, index])
                        update_copy(step, role, index).start()
        for role in (2, 1):
            for index in range(held_blocks[role]):
                block = block_of_rows(target[role], index)
                pltpu.make_async_remote_copy(
                    src_ref=us.at[step, role, index],
                    dst_ref=ur.at[step, block],
                    send_sem=u_send.at[step, role, index],
                    recv_sem=u_recv.at[step, role, index],
                    device_id=(a, source[role]),
                    device_id_type=MESH,
                ).wait_recv()

        for i in range(peers):
            if step + 1 < ITERS:
                for r in range(rows // LANES):
                    aug[i * (rows // LANES) + r] = ur[
                        step, i, :, r * LANES : (r + 1) * LANES
                    ]
            else:
                cols = slice(i * rows, (i + 1) * rows)
                out_ref[:, cols] = x_ref[:, cols] + ur[step, i].astype(f32)

    for role in (1, 2):
        for index in range(held_blocks[role]):
            rows_copy(role, index).wait_send()
    for side in range(2):
        for part in range(GAIN_PARTS):
            gain_copy_to(side, part).wait_send()
    pltpu.make_async_copy(
        zs.at[pl.ds(0, areas - 1)], zr.at[pl.ds(0, areas - 1)], z_send
    ).wait()
    for step in range(ITERS):

        @pl.when(has_lower)
        def _():
            frontier_copy(step, 0).wait_send()
            for part in range(ties // 2):
                boundary_copy(step, 0, part).wait_send()

        @pl.when(has_upper)
        def _():
            frontier_copy(step, 1).wait_send()
            for part in range(ties // 2):
                boundary_copy(step, 1, part).wait_send()

        for i in range(1, peers):
            for part in range(spread_parts):
                spread_copy(step, i, part).wait_send()
        for role in (1, 2):
            for piece in range(pieces):
                chunk_copy(step, role, piece).wait_send()
            for index in range(held_blocks[role]):
                update_copy(step, role, index).wait_send()


def on_device(
    phasor_readings,
    reading_error_spread,
    starting_voltages,
    derivative_pieces,
    derivative_tile_position,
    frontier_voltage_pieces,
    holder_line_order,
    hub_line_order,
    reciprocal_normal_operator,
):
    areas, peers = lax.axis_size("area"), lax.axis_size("snap")
    snaps, states = starting_voltages.shape
    nb = states // LANES
    mb, touched = derivative_tile_position.shape[1:]
    ties = frontier_voltage_pieces.shape[2]
    cap = holder_line_order.shape[2]
    rows = states // peers
    chunks = areas * cap // LANES
    slots = nb + 2 * ties
    all_tiles = mb * touched
    units = nb // 2
    pieces = units // 2
    f32, bf16, i32 = jnp.float32, jnp.bfloat16, jnp.int32
    vmem = pl.BlockSpec(memory_space=pltpu.VMEM)
    hbm = pl.BlockSpec(memory_space=pltpu.HBM)
    dma = pltpu.SemaphoreType.DMA
    dims = (areas, peers, snaps, nb, mb, touched, ties, cap)
    return pl.pallas_call(
        functools.partial(step_kernel, dims),
        out_shape=jax.ShapeDtypeStruct((snaps, states), f32),
        in_specs=[hbm] * 9,
        out_specs=vmem,
        scratch_shapes=[
            pltpu.VMEM((snaps, mb * LANES), f32),
            pltpu.VMEM((mb, LANES), f32),
            pltpu.VMEM((snaps, states), f32),
            pltpu.SMEM((touched, mb), i32),
            pltpu.SMEM((2, ties), i32),
            pltpu.VMEM((areas, cap), i32),
            pltpu.VMEM((areas, cap), i32),
            dma((7,)),
            pltpu.VMEM((all_tiles, LANES, LANES), bf16),
            pltpu.VMEM((3, rows, states), bf16),
            pltpu.SMEM((slots, mb), i32),
            pltpu.VMEM((2, areas, LANES), i32),
            pltpu.VMEM((areas, snaps // 2 + 1, LANES), f32),
            pltpu.VMEM((areas, snaps // 2 + 1, LANES), f32),
            pltpu.VMEM((chunks // min(chunks, 4), snaps, LANES), f32),
            pltpu.VMEM((mb, LANES), i32),
            pltpu.VMEM((mb, LANES), i32),
            pltpu.VMEM((mb, snaps, LANES), f32),
            pltpu.VMEM((mb, LANES), f32),
            pltpu.VMEM((slots + 1, snaps, LANES), bf16),
            pltpu.VMEM((ITERS, 2, ties, snaps, LANES), bf16),
            pltpu.VMEM((ITERS, 2, ties, snaps, LANES), bf16),
            pltpu.VMEM((mb, snaps, LANES), f32),
            pltpu.VMEM((ITERS, peers, mb, LANES), f32),
            pltpu.VMEM((mb, snaps, LANES), bf16),
            pltpu.VMEM((nb, snaps, LANES), f32),
            pltpu.VMEM((ITERS, 2, ties, snaps, LANES), f32),
            pltpu.VMEM((ITERS, 2, ties + 1, snaps, LANES), f32),
            pltpu.VMEM((ITERS, 3, units, snaps, 2 * LANES), bf16),
            pltpu.VMEM((ITERS, 3, 3, snaps, rows), bf16),
            pltpu.VMEM((ITERS, peers, snaps, rows), bf16),
            pltpu.VMEM((2, 3, 3, snaps, rows), f32),
            pltpu.VMEM((all_tiles + 1, snaps, LANES), f32),
            dma((2, GAIN_PARTS)),
            dma((2, GAIN_PARTS)),
            dma((2,)),
            dma((3, 3)),
            dma((3, 3)),
            dma(()),
            dma((min(chunks, 4),)),
            dma((ITERS, 2)),
            dma((ITERS, 2)),
            dma((ITERS, peers, 2)),
            dma((ITERS, peers, 2)),
            dma((ITERS, 2, ties // 2)),
            dma((ITERS, 2, ties // 2)),
            dma((ITERS, 3, pieces)),
            dma((ITERS, 3, pieces)),
            dma((ITERS, 3, 3)),
            dma((ITERS, 3, 3)),
        ],
        compiler_params=pltpu.CompilerParams(collective_id=0, has_side_effects=True),
        name="estimate",
    )(
        phasor_readings,
        reading_error_spread.reshape(mb, LANES),
        starting_voltages,
        derivative_pieces.reshape(all_tiles, LANES, LANES),
        derivative_tile_position[0].T,
        frontier_voltage_pieces[0],
        holder_line_order[0],
        hub_line_order[0],
        reciprocal_normal_operator,
    )


def solution(mesh):
    placed = (
        P("snap", "area"),
        P("area"),
        P("snap", "area"),
        P("area", None, None, None),
        P("area", None, None),
        P("area", None, None),
        P("area", None, None),
        P("area", None, None),
        P(("area", "snap"), None),
    )
    return jax.shard_map(
        on_device, mesh=mesh, in_specs=placed, out_specs=P("snap", "area"), check_vma=False
    )
```

```python
import functools

import jax
import jax.numpy as jnp
from jax import lax
from jax.experimental import pallas as pl
from jax.experimental.pallas import tpu as pltpu
from jax.sharding import PartitionSpec as P

ITERS = 2
UNROLL = (8, 8, 4)
GAIN_PARTS = 8
GAIN_EARLY = 5
LANES = 128
MESH = pl.DeviceIdType.MESH
NT = (((1,), (1,)), ((), ()))


def step_kernel(
    dims,
    z_hbm,
    var_hbm,
    x_hbm,
    tiles_hbm,
    pos_hbm,
    ties_hbm,
    holder_hbm,
    hub_hbm,
    gain_hbm,
    out_ref,
    z_ref,
    var_ref,
    x_ref,
    pos_ref,
    ties_ref,
    holder_ref,
    hub_ref,
    load_sem,
    tiles,
    gain,
    tile_index,
    table,
    zs,
    zr,
    arrived,
    inv_q,
    inv_lane,
    z_own,
    v_own,
    aug,
    fs,
    fr,
    resid,
    ssr,
    wgt,
    grads,
    bs,
    br,
    gath,
    us,
    ur,
    held,
    part_grad,
    g_send,
    g_recv,
    local_sem,
    x_send,
    x_recv,
    z_send,
    z_recv,
    f_send,
    f_recv,
    s_send,
    s_recv,
    b_send,
    b_recv,
    ring_send,
    ring_recv,
    u_send,
    u_recv,
):
    areas, peers, snaps, nb, mb, touched, ties, cap = dims
    half = snaps // 2
    chunks = areas * cap // LANES
    rows = nb * LANES // peers
    units = nb // 2
    piece_units = 2
    pieces = units // piece_units
    slots = nb + 2 * ties
    all_tiles = mb * touched
    snaps_all = snaps * peers
    f32, bf16, i32 = jnp.float32, jnp.bfloat16, jnp.int32

    a = lax.axis_index("area")
    s = lax.axis_index("snap")
    has_lower = a > 0
    has_upper = a < areas - 1

    tiles_copy = pltpu.make_async_copy(
        tiles_hbm, tiles, local_sem.at[0]
    )
    gain_copy = pltpu.make_async_copy(gain_hbm, gain.at[0], local_sem.at[1])
    loads = [
        pltpu.make_async_copy(source, target, load_sem.at[i])
        for i, (source, target) in enumerate(
            (
                (hub_hbm, hub_ref),
                (z_hbm, z_ref),
                (var_hbm, var_ref),
                (x_hbm, x_ref),
                (ties_hbm, ties_ref),
                (holder_hbm, holder_ref),
                (pos_hbm, pos_ref),
            )
        )
    ]
    for load in loads:
        load.start()

    barrier = pltpu.get_barrier_semaphore()

    def greet_area(i, carry):
        pl.semaphore_signal(
            barrier, inc=1, device_id=(lax.rem(a + i, areas), s), device_id_type=MESH
        )
        return carry

    def greet_snap(i, carry):
        pl.semaphore_signal(
            barrier, inc=1, device_id=(a, lax.rem(s + i, peers)), device_id_type=MESH
        )
        return carry

    lax.fori_loop(1, areas, greet_area, 0)
    lax.fori_loop(1, peers, greet_snap, 0)

    tiles_copy.start()
    gain_copy.start()

    for load in loads:
        load.wait()
    lane_a = lax.broadcasted_iota(i32, (areas, LANES), 1)
    for index, listing in enumerate((hub_ref, holder_ref)):
        both = jnp.concatenate([listing[...], listing[...]], axis=1)
        table[index] = both
    for block in range(nb):
        aug[block] = x_ref[:, block * LANES : (block + 1) * LANES].astype(bf16)
    aug[slots] = jnp.zeros((snaps, LANES), bf16)
    for step in range(ITERS):
        for side in range(2):
            br[step, side, ties] = jnp.zeros((snaps, LANES), f32)

    @pl.when(jnp.logical_not(has_lower))
    def _():
        for t in range(ties):
            aug[nb + t] = jnp.zeros((snaps, LANES), bf16)
            for step in range(ITERS):
                br[step, 0, t] = jnp.zeros((snaps, LANES), f32)

    @pl.when(jnp.logical_not(has_upper))
    def _():
        for t in range(ties):
            aug[nb + ties + t] = jnp.zeros((snaps, LANES), bf16)
            for step in range(ITERS):
                br[step, 1, t] = jnp.zeros((snaps, LANES), f32)

    pl.semaphore_wait(barrier, areas - 1 + peers - 1)

    def frontier_copy(step, side):
        return pltpu.make_async_remote_copy(
            src_ref=fs.at[step, side],
            dst_ref=fr.at[step, 1 - side],
            send_sem=f_send.at[step, side],
            recv_sem=f_recv.at[step, side],
            device_id=(a - 1 if side == 0 else a + 1, s),
            device_id_type=MESH,
        )

    def frontier_start(step):
        for side in range(2):
            for t in range(ties):
                entry = ties_ref[side, t]
                fs[step, side, t] = aug[jnp.where(entry >= 0, entry, slots)]

        @pl.when(has_lower)
        def _():
            frontier_copy(step, 0).start()

        @pl.when(has_upper)
        def _():
            frontier_copy(step, 1).start()

    def frontier_wait(step):
        @pl.when(has_lower)
        def _():
            frontier_copy(step, 1).wait_recv()
            for t in range(ties):
                aug[nb + t] = fr[step, 0, t]

        @pl.when(has_upper)
        def _():
            frontier_copy(step, 0).wait_recv()
            for t in range(ties):
                aug[nb + ties + t] = fr[step, 1, t]

    frontier_start(0)

    ahead = 1 - 2 * lax.rem(a, 2)

    def along(distance):
        return lax.rem(s + distance * ahead + 2 * peers, peers)

    def block_of_rows(device, index):
        shift = (0, -1, 1)[index]
        return lax.rem(device + shift * ahead + peers, peers)

    target = {1: along(3), 2: along(-2)}
    source = {1: along(-3), 2: along(2)}
    held_blocks = {0: 3, 1: 3, 2: 2}
    part_height = rows // GAIN_PARTS

    def gain_copy_to(side, part):
        where = pl.ds(part * part_height, part_height)
        return pltpu.make_async_remote_copy(
            src_ref=gain_hbm.at[where],
            dst_ref=gain.at[1 + side, where],
            send_sem=g_send.at[side, part],
            recv_sem=g_recv.at[side, part],
            device_id=(a, along(1) if side == 0 else along(-1)),
            device_id_type=MESH,
        )

    def columns_of(block):
        return pl.ds(pl.multiple_of(block * rows, rows), rows)

    def rows_copy(role, index):
        block = block_of_rows(target[role], index)
        return pltpu.make_async_remote_copy(
            src_ref=x_ref.at[:, columns_of(block)],
            dst_ref=held.at[0, role, index],
            send_sem=x_send.at[role, index],
            recv_sem=x_recv.at[role, index],
            device_id=(a, target[role]),
            device_id_type=MESH,
        )

    for role in (1, 2):
        for index in range(held_blocks[role]):
            rows_copy(role, index).start()
    for part in range(GAIN_EARLY):
        for side in range(2):
            gain_copy_to(side, part).start()
    for index in range(3):
        held[0, 0, index] = x_ref[:, columns_of(block_of_rows(s, index))]

    def table_row(index, q):
        even = table[index, pl.ds(2 * q, 1), :]
        odd = table[index, pl.ds(2 * q + 1, 1), :]
        lane = lax.broadcasted_iota(i32, (1, LANES), 1)
        return jnp.where(lane < cap, even, odd)

    lane_h = lax.broadcasted_iota(i32, (half, LANES), 1)

    wide = min(chunks, 4)
    tall = chunks // wide

    def route_out(i, carry):
        k = lax.rem(i, tall)
        turn = (k + 1) // 2
        dy = tall // 2 + turn * (1 - 2 * (k % 2))
        group = lax.div(i, tall)
        dx = lax.rem(wide // 2 + group, wide)
        chip = lax.div(a, 2)
        q = lax.rem(lax.div(chip, wide) + dy, tall) * wide + lax.rem(lax.rem(chip, wide) + dx, wide)
        where_at = table_row(0, q)
        block_of = lax.shift_right_arithmetic(where_at, 7)
        lane_of = where_at & (LANES - 1)
        lanes = jnp.broadcast_to(lane_of, (snaps, LANES))
        from_block = jnp.broadcast_to(block_of, (snaps, LANES))
        taken = jnp.zeros((snaps, LANES), f32)
        for block in range(mb):
            found = jnp.take_along_axis(
                z_ref[:, block * LANES : (block + 1) * LANES], lanes, axis=1
            )
            taken = jnp.where(from_block == block, found, taken)
        low, high = taken[:half], taken[half:]
        zs[2 * q, pl.ds(0, half)] = jnp.where(lane_h < cap, low, pltpu.roll(high, cap, 1))
        zs[2 * q + 1, pl.ds(0, half)] = jnp.where(lane_h < cap, pltpu.roll(low, cap, 1), high)
        var_found = jnp.take_along_axis(
            var_ref[...], jnp.broadcast_to(lane_of, (mb, LANES)), axis=1
        )
        var_rows = lax.broadcasted_iota(i32, (mb, LANES), 0)
        var_row = jnp.sum(
            jnp.where(var_rows == jnp.broadcast_to(block_of, (mb, LANES)), var_found, 0.0),
            axis=0,
            keepdims=True,
        )
        for parity in range(2):
            d = 2 * q + parity
            zs[d, pl.ds(half, 1)] = var_row

            @pl.when(d != a)
            def _():
                pltpu.make_async_remote_copy(
                    src_ref=zs.at[d],
                    dst_ref=zr.at[a],
                    send_sem=z_send,
                    recv_sem=z_recv.at[group],
                    device_id=(d, s),
                    device_id_type=MESH,
                ).start()

            @pl.when(d == a)
            def _():
                pltpu.make_async_copy(zs.at[d], zr.at[a], z_recv.at[group]).start()

        return carry

    lax.fori_loop(0, chunks, route_out, 0, unroll=UNROLL[2])

    sub_q = lax.broadcasted_iota(i32, (mb, LANES), 0)
    lane_q = lax.broadcasted_iota(i32, (mb, LANES), 1)
    sub_l = lax.broadcasted_iota(i32, (LANES, LANES), 0)

    def invert(q, total):
        where_at = table_row(1, q)
        mine = jnp.broadcast_to(lax.shift_right_arithmetic(where_at, 7), (mb, LANES)) == sub_q
        left = jnp.concatenate(
            [jnp.where(mine, lane_q, 0).astype(f32), jnp.where(mine, q, 0).astype(f32)], axis=0
        ).astype(bf16)
        hit = jnp.broadcast_to(where_at & (LANES - 1), (LANES, LANES)) == sub_l
        right = jnp.where(hit, 1.0, 0.0).astype(bf16)
        return total + lax.dot_general(left, right, NT, preferred_element_type=f32)

    inverse = lax.fori_loop(
        0, chunks, invert, jnp.zeros((2 * mb, LANES), f32), unroll=UNROLL[0]
    )
    inv_lane[...] = inverse[:mb].astype(i32) & (LANES - 1)
    inv_q[...] = inverse[mb:].astype(i32)

    def index_tiles(n, carry):
        for j in range(mb):
            which = all_tiles
            for k in range(touched):
                tile = j * touched + k
                which = jnp.where(pos_ref[k, j] == n, tile, which)
            tile_index[n, j] = which
        return carry

    tiles_copy.wait()

    def predict(mine):
        def body(j, carry):
            total = jnp.zeros((snaps, LANES), f32)
            for k in range(touched):
                total += lax.dot_general(
                    aug[pos_ref[k, j]],
                    tiles[j * touched + k],
                    NT,
                    preferred_element_type=f32,
                )
            resid[j] = total
            return carry

        lax.fori_loop(mine.start, mine.stop, body, 0, unroll=min(len(mine), UNROLL[1]))

    frontier_wait(0)
    predict(range(mb))
    lax.fori_loop(0, slots, index_tiles, 0)
    part_grad[all_tiles] = jnp.zeros((snaps, LANES), f32)
    gain_copy.wait()

    my_wide = lax.rem(lax.div(a, 2), wide)
    batch = zr.at[pl.ds(0, 2 * tall)]
    sub_v = lax.broadcasted_iota(i32, (2 * tall, LANES), 0)
    my_half = lax.rem(a, 2) * cap
    for group in range(wide):
        from_wide = lax.rem(my_wide + 2 * wide - (wide // 2 + group) % wide, wide)
        pltpu.make_async_copy(batch, batch, z_recv.at[group]).wait()
        variances = jnp.concatenate(
            [
                zr[2 * (row * wide + from_wide) + parity, pl.ds(half, 1)]
                for row in range(tall)
                for parity in range(2)
            ],
            axis=0,
        )

        def unpack(row, carry):
            q = row * wide + from_wide
            even, odd = zr[2 * q, pl.ds(0, half)], zr[2 * q + 1, pl.ds(0, half)]
            arrived[row, pl.ds(0, half)] = jnp.where(
                lane_h < cap, even, pltpu.roll(odd, cap, 1)
            )
            arrived[row, pl.ds(half, half)] = jnp.where(
                lane_h < cap, pltpu.roll(even, cap, 1), odd
            )
            return carry

        lax.fori_loop(0, tall, unpack, 0, unroll=True)

        def reorder(j, carry):
            lanes = jnp.broadcast_to(inv_lane[pl.ds(j, 1), :], (snaps, LANES))
            from_chunk = jnp.broadcast_to(inv_q[pl.ds(j, 1), :], (snaps, LANES))
            taken = jnp.zeros((snaps, LANES), f32) if group == 0 else z_own[j]
            for row in range(tall):
                found = jnp.take_along_axis(arrived[row], lanes, axis=1)
                taken = jnp.where(from_chunk == row * wide + from_wide, found, taken)
            z_own[j] = taken
            lane_of = inv_lane[pl.ds(j, 1), :]
            chunk_of = inv_q[pl.ds(j, 1), :]
            place = 2 * lax.shift_right_arithmetic(chunk_of, wide.bit_length() - 1)
            place += lax.shift_right_arithmetic(lane_of, 6)
            place = jnp.where((chunk_of & (wide - 1)) == from_wide, place, -1)
            found = jnp.take_along_axis(
                variances,
                jnp.broadcast_to((lane_of & (cap - 1)) + my_half, (2 * tall, LANES)),
                axis=1,
            )
            part = jnp.sum(
                jnp.where(jnp.broadcast_to(place, (2 * tall, LANES)) == sub_v, found, 0.0),
                axis=0,
                keepdims=True,
            )
            v_own[pl.ds(j, 1), :] = part if group == 0 else v_own[pl.ds(j, 1), :] + part
            return carry

        lax.fori_loop(0, mb, reorder, 0, unroll=min(mb, 4))

    spread_parts = 2 if mb % 16 == 0 else 1
    part_rows = mb // spread_parts

    def spread_copy(step, i, part):
        where = pl.ds(part * part_rows, part_rows)
        peer = lax.rem(s + i, peers)
        return pltpu.make_async_remote_copy(
            src_ref=ssr.at[step, s, where],
            dst_ref=ssr.at[step, s, where],
            send_sem=s_send.at[step, i, part],
            recv_sem=s_recv.at[step, s, part],
            device_id=(a, peer),
            device_id_type=MESH,
        )

    def spread_wait(step, i, part):
        source = lax.rem(s + i, peers)
        where = pl.ds(part * part_rows, part_rows)
        pltpu.make_async_remote_copy(
            src_ref=ssr.at[step, source, where],
            dst_ref=ssr.at[step, source, where],
            send_sem=s_send.at[step, i, part],
            recv_sem=s_recv.at[step, source, part],
            device_id=(a, source),
            device_id_type=MESH,
        ).wait_recv()

    def boundary_copy(step, side, part):
        return pltpu.make_async_remote_copy(
            src_ref=bs.at[step, side, pl.ds(2 * part, 2)],
            dst_ref=br.at[step, 1 - side, pl.ds(2 * part, 2)],
            send_sem=b_send.at[step, side, part],
            recv_sem=b_recv.at[step, side, part],
            device_id=(a - 1 if side == 0 else a + 1, s),
            device_id_type=MESH,
        )

    def chunk_copy(step, role, piece):
        part = pl.ds(piece * piece_units, piece_units)
        return pltpu.make_async_remote_copy(
            src_ref=gath.at[step, 0, part],
            dst_ref=gath.at[step, role, part],
            send_sem=ring_send.at[step, role, piece],
            recv_sem=ring_recv.at[step, role, piece],
            device_id=(a, target[role]),
            device_id_type=MESH,
        )

    def update_copy(step, role, index):
        return pltpu.make_async_remote_copy(
            src_ref=us.at[step, role, index],
            dst_ref=ur.at[step, block_of_rows(s, index)],
            send_sem=u_send.at[step, role, index],
            recv_sem=u_recv.at[step, role, index],
            device_id=(a, source[role]),
            device_id_type=MESH,
        )

    def tile_products(mine):
        def body(j, carry):
            for k in range(0, touched, 2):
                pair = jnp.dot(
                    wgt[j],
                    jnp.concatenate(
                        [tiles[j * touched + k], tiles[j * touched + k + 1]], axis=1
                    ),
                    preferred_element_type=f32,
                )
                part_grad[j * touched + k] = pair[:, :LANES]
                part_grad[j * touched + k + 1] = pair[:, LANES:]
            return carry

        lax.fori_loop(mine.start, mine.stop, body, 0, unroll=min(len(mine), 8))

    def slot_sum(n):
        terms = [part_grad[tile_index[n, j]] for j in range(mb)]
        while len(terms) > 1:
            terms = [
                terms[i] + terms[i + 1] if i + 1 < len(terms) else terms[i]
                for i in range(0, len(terms), 2)
            ]
        return terms[0]

    def gain_piece(step, role, piece, sums):
        for index in range(held_blocks[role]):
            for u in range(piece * piece_units, (piece + 1) * piece_units):
                part = lax.dot_general(
                    gath[step, role, u],
                    gain[index, :, u * 2 * LANES : (u + 1) * 2 * LANES],
                    NT,
                    preferred_element_type=f32,
                )
                sums[role, index] = sums[role, index] + part if (role, index) in sums else part

    def returned(step, role, index, update):
        if step + 1 < ITERS:
            held[1, role, index] = update
            return (held[0, role, index] + update).astype(bf16)
        return (held[1, role, index] + update).astype(bf16)

    for step in range(ITERS):
        if step > 0:
            frontier_start(step)
            frontier_wait(step)
        for part in range(spread_parts):
            mine = range(part * part_rows, (part + 1) * part_rows)
            if step > 0:
                predict(mine)
            for j in mine:
                left_over = z_own[j] - resid[j]
                resid[j] = left_over
                ssr[step, s, pl.ds(j, 1), :] = jnp.sum(
                    left_over * left_over, axis=0, keepdims=True
                )
            for i in range(1, peers):
                spread_copy(step, i, part).start()
        if step == 0:
            for part in range(GAIN_EARLY, GAIN_PARTS):
                for side in range(2):
                    gain_copy_to(side, part).start()
        for part in range(spread_parts):
            mine = range(part * part_rows, (part + 1) * part_rows)
            for i in range(1, peers):
                spread_wait(step, i, part)
            where = pl.ds(part * part_rows, part_rows)
            total = ssr[step, 0, where]
            for i in range(1, peers):
                total += ssr[step, i, where]
            scale = v_own[where, :] + total / snaps_all
            for j in mine:
                row = j - part * part_rows
                wgt[j] = (resid[j] / scale[row : row + 1, :]).astype(bf16)
            tile_products(mine)
        for side in range(2):
            for part in range(ties // 2):
                for t in (2 * part, 2 * part + 1):
                    bs[step, side, t] = slot_sum(nb + side * ties + t)

                @pl.when(has_lower if side == 0 else has_upper)
                def _():
                    boundary_copy(step, side, part).start()

        def own_slots(n, carry):
            grads[n] = slot_sum(n)
            return carry

        lax.fori_loop(0, nb, own_slots, 0, unroll=4)

        @pl.when(has_upper)
        def _():
            for part in range(ties // 2):
                boundary_copy(step, 0, part).wait_recv()

        @pl.when(has_lower)
        def _():
            for part in range(ties // 2):
                boundary_copy(step, 1, part).wait_recv()

        for piece in range(pieces):
            for block in range(2 * piece_units * piece, 2 * piece_units * (piece + 1)):
                total = grads[block]
                for side in range(2):
                    which = ties
                    for t in range(ties):
                        which = jnp.where(ties_ref[side, t] == block, t, which)
                    total += br[step, side, which]
                first = (block % 2) * LANES
                gath[step, 0, block // 2, :, first : first + LANES] = total.astype(bf16)
            for role in (1, 2):
                chunk_copy(step, role, piece).start()

        if step == 0:
            for side in range(2):
                for part in range(GAIN_PARTS):
                    gain_copy_to(side, part).wait_recv()
            for role in (1, 2):
                for index in range(held_blocks[role]):
                    rows_copy(role, index).wait_recv()
        sums = {}
        for piece in range(pieces):
            gain_piece(step, 0, piece, sums)
        for index in range(3):
            ur[step, block_of_rows(s, index)] = returned(step, 0, index, sums[0, index])
        for piece in range(pieces):
            for role in (2, 1):
                chunk_copy(step, role, piece).wait_recv()
                gain_piece(step, role, piece, sums)
                if piece + 1 == pieces:
                    for index in range(held_blocks[role]):
                        us[step, role, index] = returned(step, role, index, sums[role, index])
                        update_copy(step, role, index).start()
        for role in (2, 1):
            for index in range(held_blocks[role]):
                block = block_of_rows(target[role], index)
                pltpu.make_async_remote_copy(
                    src_ref=us.at[step, role, index],
                    dst_ref=ur.at[step, block],
                    send_sem=u_send.at[step, role, index],
                    recv_sem=u_recv.at[step, role, index],
                    device_id=(a, source[role]),
                    device_id_type=MESH,
                ).wait_recv()

        for i in range(peers):
            if step + 1 < ITERS:
                for r in range(rows // LANES):
                    aug[i * (rows // LANES) + r] = ur[
                        step, i, :, r * LANES : (r + 1) * LANES
                    ]
            else:
                cols = slice(i * rows, (i + 1) * rows)
                out_ref[:, cols] = x_ref[:, cols] + ur[step, i].astype(f32)

    for role in (1, 2):
        for index in range(held_blocks[role]):
            rows_copy(role, index).wait_send()
    for side in range(2):
        for part in range(GAIN_PARTS):
            gain_copy_to(side, part).wait_send()
    pltpu.make_async_copy(
        zs.at[pl.ds(0, areas - 1)], zr.at[pl.ds(0, areas - 1)], z_send
    ).wait()
    for step in range(ITERS):

        @pl.when(has_lower)
        def _():
            frontier_copy(step, 0).wait_send()
            for part in range(ties // 2):
                boundary_copy(step, 0, part).wait_send()

        @pl.when(has_upper)
        def _():
            frontier_copy(step, 1).wait_send()
            for part in range(ties // 2):
                boundary_copy(step, 1, part).wait_send()

        for i in range(1, peers):
            for part in range(spread_parts):
                spread_copy(step, i, part).wait_send()
        for role in (1, 2):
            for piece in range(pieces):
                chunk_copy(step, role, piece).wait_send()
            for index in range(held_blocks[role]):
                update_copy(step, role, index).wait_send()


def on_device(
    phasor_readings,
    reading_error_spread,
    starting_voltages,
    derivative_pieces,
    derivative_tile_position,
    frontier_voltage_pieces,
    holder_line_order,
    hub_line_order,
    reciprocal_normal_operator,
):
    areas, peers = lax.axis_size("area"), lax.axis_size("snap")
    snaps, states = starting_voltages.shape
    nb = states // LANES
    mb, touched = derivative_tile_position.shape[1:]
    ties = frontier_voltage_pieces.shape[2]
    cap = holder_line_order.shape[2]
    rows = states // peers
    chunks = areas * cap // LANES
    slots = nb + 2 * ties
    all_tiles = mb * touched
    units = nb // 2
    pieces = units // 2
    f32, bf16, i32 = jnp.float32, jnp.bfloat16, jnp.int32
    vmem = pl.BlockSpec(memory_space=pltpu.VMEM)
    hbm = pl.BlockSpec(memory_space=pltpu.HBM)
    dma = pltpu.SemaphoreType.DMA
    dims = (areas, peers, snaps, nb, mb, touched, ties, cap)
    return pl.pallas_call(
        functools.partial(step_kernel, dims),
        out_shape=jax.ShapeDtypeStruct((snaps, states), f32),
        in_specs=[hbm] * 9,
        out_specs=vmem,
        scratch_shapes=[
            pltpu.VMEM((snaps, mb * LANES), f32),
            pltpu.VMEM((mb, LANES), f32),
            pltpu.VMEM((snaps, states), f32),
            pltpu.SMEM((touched, mb), i32),
            pltpu.SMEM((2, ties), i32),
            pltpu.VMEM((areas, cap), i32),
            pltpu.VMEM((areas, cap), i32),
            dma((7,)),
            pltpu.VMEM((all_tiles, LANES, LANES), bf16),
            pltpu.VMEM((3, rows, states), bf16),
            pltpu.SMEM((slots, mb), i32),
            pltpu.VMEM((2, areas, LANES), i32),
            pltpu.VMEM((areas, snaps // 2 + 1, LANES), f32),
            pltpu.VMEM((areas, snaps // 2 + 1, LANES), f32),
            pltpu.VMEM((chunks // min(chunks, 4), snaps, LANES), f32),
            pltpu.VMEM((mb, LANES), i32),
            pltpu.VMEM((mb, LANES), i32),
            pltpu.VMEM((mb, snaps, LANES), f32),
            pltpu.VMEM((mb, LANES), f32),
            pltpu.VMEM((slots + 1, snaps, LANES), bf16),
            pltpu.VMEM((ITERS, 2, ties, snaps, LANES), bf16),
            pltpu.VMEM((ITERS, 2, ties, snaps, LANES), bf16),
            pltpu.VMEM((mb, snaps, LANES), f32),
            pltpu.VMEM((ITERS, peers, mb, LANES), f32),
            pltpu.VMEM((mb, snaps, LANES), bf16),
            pltpu.VMEM((nb, snaps, LANES), f32),
            pltpu.VMEM((ITERS, 2, ties, snaps, LANES), f32),
            pltpu.VMEM((ITERS, 2, ties + 1, snaps, LANES), f32),
            pltpu.VMEM((ITERS, 3, units, snaps, 2 * LANES), bf16),
            pltpu.VMEM((ITERS, 3, 3, snaps, rows), bf16),
            pltpu.VMEM((ITERS, peers, snaps, rows), bf16),
            pltpu.VMEM((2, 3, 3, snaps, rows), f32),
            pltpu.VMEM((all_tiles + 1, snaps, LANES), f32),
            dma((2, GAIN_PARTS)),
            dma((2, GAIN_PARTS)),
            dma((2,)),
            dma((3, 3)),
            dma((3, 3)),
            dma(()),
            dma((min(chunks, 4),)),
            dma((ITERS, 2)),
            dma((ITERS, 2)),
            dma((ITERS, peers, 2)),
            dma((ITERS, peers, 2)),
            dma((ITERS, 2, ties // 2)),
            dma((ITERS, 2, ties // 2)),
            dma((ITERS, 3, pieces)),
            dma((ITERS, 3, pieces)),
            dma((ITERS, 3, 3)),
            dma((ITERS, 3, 3)),
        ],
        compiler_params=pltpu.CompilerParams(collective_id=0, has_side_effects=True),
        name="estimate",
    )(
        phasor_readings,
        reading_error_spread.reshape(mb, LANES),
        starting_voltages,
        derivative_pieces.reshape(all_tiles, LANES, LANES),
        derivative_tile_position[0].T,
        frontier_voltage_pieces[0],
        holder_line_order[0],
        hub_line_order[0],
        reciprocal_normal_operator,
    )


def solution(mesh):
    placed = (
        P("snap", "area"),
        P("area"),
        P("snap", "area"),
        P("area", None, None, None),
        P("area", None, None),
        P("area", None, None),
        P("area", None, None),
        P("area", None, None),
        P(("area", "snap"), None),
    )
    return jax.shard_map(
        on_device, mesh=mesh, in_specs=placed, out_specs=P("snap", "area"), check_vma=False
    )
```
